128 devices in a mesh: row: 16 (over z, y), col: 8 (over x, core).
Axes of the slice: x: 4, y: 4, z: 4, core: 2. Of those that a mesh axis runs over, the one named last changes fastest.
Arguments:
- patches: bfloat16 [128, 128, 384], P('row', 'col'), may hold values from -10 to 10
- tissue: int32 [128, 128], P('row', 'col'), may hold values from 0 to 1
- in_weight: bfloat16 [384, 1536], replicated, may hold values from -0.3125 to 0.3125
- conv_weight: float32 [3, 3, 768], replicated, may hold values from -2 to 2
- conv_bias: float32 [768], replicated, may hold values from -3 to 3
- x_weight: bfloat16 [768, 224], replicated, may hold values from -0.21875 to 0.21875
- dt_weight: bfloat16 [4, 24, 768], replicated, may hold values from -1.25 to 1.25
- dt_bias: float32 [4, 768], replicated, may hold values from -5.5 to -3.5
- decay_rate: float32 [4, 768, 16], replicated, may hold values from 0.0001 to 4
- skip_gain: float32 [768], replicated, may hold values from 0.5 to 2
- norm_gain: float32 [768], replicated, may hold values from 0.1 to 1.9
- out_weight: bfloat16 [768, 384], replicated, may hold values from -0.21875 to 0.21875
Outputs:
- result: bfloat16 [128, 128, 384], P('row', 'col')
The draws below stay inside these ranges and needn't reach their ends.
All inputs are finite; a program needn't handle non-finite values.
Results may differ from the reference program's by a relative error of at most 0.0076.
Values may be sent and summed in bfloat16 or wider, within the bound.
No kernel may reach another device: no remote copies, remote signals or barrier semaphores. Data moves between devices by JAX's collectives and lax.ppermute only.
A program may use at most 256 MiB of HBM per device.

```python
import math
import jax
import jax.numpy as jnp
from jax import lax

CH = 384
INNER = 768
STATE = 16
RANK = 24
IMG_H = 128
IMG_W = 128


def draw_patches(key, part):
    base_key = jax.random.fold_in(key, 101)
    key_noise, key_rows, key_cols = jax.random.split(base_key, 3)
    noise_part = jnp.clip(jax.random.normal(key_noise, (IMG_H, IMG_W, CH), jnp.float32), -4.0, 4.0)
    spread = math.log(2.0)
    row_scale = jnp.exp(jax.random.uniform(key_rows, (IMG_H, 1, 1), jnp.float32, -spread, spread))
    col_scale = jnp.exp(jax.random.uniform(key_cols, (1, IMG_W, 1), jnp.float32, -spread, spread))
    values = noise_part * row_scale * col_scale
    return jnp.clip(values, -10.0, 10.0).astype(jnp.bfloat16)


def draw_tissue(key, part):
    base_key = jax.random.fold_in(key, 202)
    key_rows, key_cols, key_cells = jax.random.split(base_key, 3)
    row_live = jax.random.randint(key_rows, (IMG_H, 1), 0, 4) > 0
    col_live = jax.random.randint(key_cols, (1, IMG_W), 0, 4) > 0
    cell_live = jax.random.randint(key_cells, (IMG_H, IMG_W), 0, 8) > 0
    return jnp.logical_and(jnp.logical_and(row_live, col_live), cell_live).astype(jnp.int32)


def bell_draw(stream_key, dims, deviation, most, held_as=jnp.bfloat16):
    drawn = jax.random.normal(stream_key, dims, jnp.float32) * deviation
    return jnp.minimum(jnp.maximum(drawn, -most), most).astype(held_as)


def setup_inputs(seed: int = 0) -> dict:
    arg_keys = jax.random.split(jax.random.key(seed), 13)
    patches = draw_patches(jax.random.fold_in(arg_keys[12], 71), 0)
    tissue = draw_tissue(jax.random.fold_in(arg_keys[12], 71), 0)
    in_weight = bell_draw(arg_keys[2], (CH, 2 * INNER), CH ** -0.5, 0.3125)
    conv_weight = bell_draw(arg_keys[3], (3, 3, INNER), 9 ** -0.5, 2.0, jnp.float32)
    conv_bias = bell_draw(arg_keys[4], (INNER,), 0.5, 3.0, jnp.float32)
    x_weight = bell_draw(arg_keys[5], (INNER, 4 * (RANK + 2 * STATE)), INNER ** -0.5, 0.21875)
    dt_weight = bell_draw(arg_keys[6], (4, RANK, INNER), RANK ** -0.5, 1.25)
    dt_bias = jnp.clip(jax.random.uniform(arg_keys[7], (4, INNER), jnp.float32, -5.5, -3.5), -5.5, -3.5)
    decay_rate = jnp.clip(jnp.exp(jax.random.uniform(arg_keys[8], (4, INNER, STATE), jnp.float32, math.log(0.0001), math.log(4.0))), 0.0001, 4.0)
    skip_gain = jnp.clip(jax.random.uniform(arg_keys[9], (INNER,), jnp.float32, 0.5, 2.0), 0.5, 2.0)
    norm_gain = jnp.clip(1.0 + 0.18 * jax.random.normal(arg_keys[10], (INNER,), jnp.float32), 0.1, 1.9)
    out_weight = bell_draw(arg_keys[11], (INNER, CH), INNER ** -0.5, 0.21875)
    return dict(patches=patches, tissue=tissue, in_weight=in_weight, conv_weight=conv_weight, conv_bias=conv_bias, x_weight=x_weight, dt_weight=dt_weight, dt_bias=dt_bias, decay_rate=decay_rate, skip_gain=skip_gain, norm_gain=norm_gain, out_weight=out_weight)


def to_order(values, columns_first, backward):
    grid = values.reshape(IMG_H, IMG_W, -1)
    if columns_first:
        grid = jnp.transpose(grid, (1, 0, 2))
    series = grid.reshape(IMG_H * IMG_W, -1)
    if backward:
        series = series[::-1]
    return series

def from_order(series, columns_first, backward):
    if backward:
        series = series[::-1]
    if columns_first:
        grid = jnp.transpose(series.reshape(IMG_W, IMG_H, -1), (1, 0, 2))
    else:
        grid = series.reshape(IMG_H, IMG_W, -1)
    return grid.reshape(IMG_H * IMG_W, -1)

def selective(steps_dt, inputs_du, b_coeffs, c_coeffs, decays):

    def advance(carried, inputs):
        delta, driven, b_row, c_row = inputs
        carried = jnp.exp(-decays * delta[:, None]) * carried + driven[:, None] * b_row[None, :]
        return (carried, lax.optimization_barrier(jnp.sum(carried * c_row[None, :], axis=1)))
    start = jnp.zeros((INNER, STATE), jnp.float32)
    final_state, outputs = lax.scan(advance, start, (steps_dt, inputs_du, b_coeffs, c_coeffs))
    return outputs

def reference(patches, tissue, in_weight, conv_weight, conv_bias, x_weight, dt_weight, dt_bias, decay_rate, skip_gain, norm_gain, out_weight):
    token_count = IMG_H * IMG_W
    flattened = patches.reshape(token_count, CH)
    projected = jnp.dot(flattened, in_weight, preferred_element_type=jnp.float32)
    x_inner = projected[:, :INNER].astype(jnp.bfloat16).reshape(IMG_H, IMG_W, INNER)
    gate_half = projected[:, INNER:].astype(jnp.bfloat16)
    framed = jnp.pad(x_inner.astype(jnp.float32), ((1, 1), (1, 1), (0, 0)))
    conv_sum = jnp.zeros((IMG_H, IMG_W, INNER), jnp.float32) + conv_bias
    for offset_row in range(3):
        for offset_col in range(3):
            conv_sum = conv_sum + framed[offset_row:offset_row + IMG_H, offset_col:offset_col + IMG_W] * conv_weight[offset_row, offset_col]
    activated = jax.nn.silu(conv_sum).astype(jnp.bfloat16).reshape(token_count, INNER)
    scan_proj = jnp.dot(activated, x_weight, preferred_element_type=jnp.float32)
    tissue_live = tissue.reshape(token_count, 1).astype(jnp.float32)
    activated_wide = activated.astype(jnp.float32)
    width_each = RANK + 2 * STATE
    combined = jnp.zeros((token_count, INNER), jnp.float32)
    for direction in range(4):
        section = scan_proj[:, direction * width_each:(direction + 1) * width_each]
        low_rank = section[:, :RANK].astype(jnp.bfloat16)
        steps_dt = jax.nn.softplus(jnp.dot(low_rank, dt_weight[direction], preferred_element_type=jnp.float32) + dt_bias[direction]) * tissue_live
        inputs_du = steps_dt * activated_wide
        b_coeffs = section[:, RANK:RANK + STATE]
        c_coeffs = section[:, RANK + STATE:]
        columns_first = direction >= 2
        backward = direction % 2 == 1
        ordered = [to_order(member, columns_first, backward) for member in (steps_dt, inputs_du, b_coeffs, c_coeffs)]
        outputs = selective(ordered[0], ordered[1], ordered[2], ordered[3], decay_rate[direction])
        combined = combined + from_order(outputs, columns_first, backward)
    combined = combined + skip_gain * activated_wide
    mean_value = lax.optimization_barrier(jnp.mean(combined, axis=1, keepdims=True))
    centered = combined - mean_value
    variance = lax.optimization_barrier(jnp.mean(centered * centered, axis=1, keepdims=True))
    normed = centered * lax.rsqrt(variance + 1e-05) * norm_gain
    mixed = (normed * jax.nn.silu(gate_half.astype(jnp.float32))).astype(jnp.bfloat16)
    result = jnp.dot(mixed, out_weight, preferred_element_type=jnp.float32) * tissue_live
    return result.astype(jnp.bfloat16).reshape(IMG_H, IMG_W, CH)
```

```python
import functools
import math

import jax
import jax.numpy as jnp
from jax import lax
from jax.experimental import pallas as pl
from jax.experimental.pallas import tpu as pltpu
from jax.sharding import PartitionSpec as P

F32 = jnp.float32
BF16 = jnp.bfloat16
LANES = 128
SLICE = 96
STATE = 16
RANK = 24
EACH = RANK + 2 * STATE
OFF_LANE = 2 * EACH
TOT = 24
LOG2E = math.log2(math.e)


def vmem(count):
    return [pl.BlockSpec(memory_space=pltpu.VMEM)] * count


def call(kernel, out_shape, in_specs, scratch=(), flops=10**7, name=None):
    return pl.pallas_call(
        kernel,
        out_shape=out_shape,
        in_specs=in_specs,
        out_specs=jax.tree.map(lambda _: pl.BlockSpec(memory_space=pltpu.VMEM), out_shape),
        scratch_shapes=list(scratch),
        compiler_params=pltpu.CompilerParams(vmem_limit_bytes=48 << 20),
        cost_estimate=pl.CostEstimate(flops=flops, bytes_accessed=4 * 10**6, transcendentals=0),
        name=name,
    )


def lane_iota(shape):
    return lax.broadcasted_iota(jnp.int32, shape, len(shape) - 1)


def softplus(x):
    return jnp.maximum(x, 0.0) + jnp.log1p(jnp.exp(-jnp.abs(x)))


def silu(x):
    return x * jax.nn.sigmoid(x)


def cut_slice(values, k):
    j0, off = divmod(SLICE * k, LANES)
    first = values[:, j0 * LANES : (j0 + 1) * LANES]
    if off == 0:
        return first
    shift = LANES - off
    head = pltpu.roll(first, shift, 1)
    if shift >= SLICE:
        return head
    second = values[:, (j0 + 1) * LANES : (j0 + 2) * LANES]
    tail = pltpu.roll(second, shift, 1)
    return jnp.where(lane_iota(head.shape) < shift, head, tail)


def join_slices(parts):
    tiles = []
    lane = lane_iota(parts[0].shape)
    for m in range(2):
        y0, y1, y2, y3 = parts[4 * m : 4 * m + 4]
        r1 = pltpu.roll(y1, 96, 1)
        r2 = pltpu.roll(y2, 64, 1)
        r3 = pltpu.roll(y3, 32, 1)
        tiles.append(jnp.where(lane < 96, y0, r1))
        tiles.append(jnp.where(lane < 64, r1, r2))
        tiles.append(jnp.where(lane < 32, r2, r3))
    return tiles


def order_matrix(to_columns):
    q = lax.broadcasted_iota(jnp.int32, (LANES, LANES), 0 if to_columns else 1)
    p = lax.broadcasted_iota(jnp.int32, (LANES, LANES), 1 if to_columns else 0)
    return (p == (q % 8) * 16 + q // 8).astype(F32).astype(BF16)


def local_kernel(
    x_ref, top_ref, bottom_ref, left_ref, right_ref, w_ref, cw_ref, cb_ref, xw_ref, off_ref,
    act_ref, recr_ref, recc_ref, frame_ref,
):
    inner = x_ref.shape[1]
    weight = w_ref[...]

    def project(v):
        return jnp.dot(v, weight, preferred_element_type=F32).astype(BF16).astype(F32)

    frame_ref[1:9, 8:24, :] = x_ref[...].astype(F32).reshape(8, 16, inner)
    frame_ref[0:1, 8:24, :] = project(top_ref[...]).reshape(1, 16, inner)
    frame_ref[9:10, 8:24, :] = project(bottom_ref[...]).reshape(1, 16, inner)
    left = project(left_ref[...])
    right = project(right_ref[...])
    for i in range(10):
        frame_ref[i, 7:8, :] = left[i : i + 1]
        frame_ref[i, 24:25, :] = right[i : i + 1]
    total = jnp.zeros((8, 16, inner), F32) + cb_ref[...].reshape(1, 1, inner)
    for dc in range(3):
        for dr in range(3):
            k = dr * 3 + dc
            total = total + frame_ref[dr : dr + 8, 7 + dc : 23 + dc, :] * cw_ref[
                k : k + 1, :
            ].reshape(1, 1, inner)
    act = silu(total).reshape(LANES, inner).astype(BF16)
    act_ref[...] = act
    coef = jnp.dot(act, xw_ref[...], preferred_element_type=F32)
    lane = lane_iota((LANES, LANES))
    off = jnp.broadcast_to(off_ref[...], (LANES, LANES))
    coef_r = jnp.where(lane == OFF_LANE, off, coef[:, :LANES]).astype(BF16)
    coef_c = jnp.where(lane == OFF_LANE, off, coef[:, LANES:]).astype(BF16)
    turn = order_matrix(True)
    act_r = jnp.dot(turn, act, preferred_element_type=F32)
    coef_r = jnp.dot(turn, coef_r, preferred_element_type=F32).astype(BF16)
    wide = act.astype(F32)
    half = coef_c.astype(F32).reshape(8, 16, LANES)
    halves = [
        half[:, 8 * h : 8 * h + 8, :].reshape(64, LANES).astype(BF16) for h in range(2)
    ]
    for k in range(8):
        recr_ref[k, :, :LANES] = cut_slice(act_r, k).astype(BF16)
        recr_ref[k, :, LANES:] = coef_r
        piece = cut_slice(wide, k).reshape(8, 16, LANES)
        for h in range(2):
            recc_ref[2 * k + h, :, :LANES] = (
                piece[:, 8 * h : 8 * h + 8, :].reshape(64, LANES).astype(BF16)
            )
            recc_ref[2 * k + h, :, LANES:] = halves[h]


def unpack(rec_ref, du_ref, coef_ref, dt_ref):
    act = rec_ref[:, :LANES].astype(F32)
    for o in range(2):
        du_ref[o] = dt_ref[o] * act
    coef_ref[...] = rec_ref[:, LANES:].astype(F32)


def totals_kernel(copies, rec_ref, dtw_ref, bias_ref, decay_ref, dt_ref, excl_ref, tot_ref, du_ref, coef_ref):
    steps = rec_ref.shape[0] // 8
    coef_bf = rec_ref[:, LANES:]
    for o in range(2):
        z = jnp.dot(coef_bf, dtw_ref[o], preferred_element_type=F32) + bias_ref[o]
        dt_ref[o] = softplus(z)
    unpack(rec_ref, du_ref, coef_ref, dt_ref)
    sub = lax.broadcasted_iota(jnp.int32, (8, LANES), 0)
    for o in range(2):
        decay = [jnp.broadcast_to(decay_ref[o, n : n + 1, :], (8, LANES)) for n in range(STATE)]

        def advance(t, carry):
            span, states = carry
            t = steps - 1 - t if o == 1 else t
            at = pl.ds(pl.multiple_of(t * 8, 8), 8)
            dt = dt_ref[o, at, :]
            du = du_ref[o, at, :]
            coef = coef_ref[at, :]
            new = []
            for n in range(STATE):
                lane = o * EACH + RANK + n
                b = jnp.broadcast_to(coef[:, lane : lane + 1], (8, LANES))
                new.append(jnp.exp2(decay[n] * dt) * states[n] + du * b)
            return span + dt, tuple(new)

        zero = jnp.zeros((8, LANES), F32)
        span, states = lax.fori_loop(0, steps, advance, (zero, (zero,) * STATE), unroll=2)
        states = list(states)
        for k in (1, 2, 4):
            shift = k if o == 0 else 8 - k
            keep = sub >= k if o == 0 else sub < 8 - k
            for n in range(STATE):
                moved = jnp.where(keep, pltpu.roll(states[n], shift, 0), 0.0)
                states[n] = jnp.exp2(decay[n] * span) * moved + states[n]
            span = span + jnp.where(keep, pltpu.roll(span, shift, 0), 0.0)
        shift = 1 if o == 0 else 7
        keep = sub >= 1 if o == 0 else sub < 7
        last = 7 if o == 0 else 0
        for n in range(STATE):
            excl_ref[o, n] = jnp.where(keep, pltpu.roll(states[n], shift, 0), 0.0)
            for k in range(copies):
                tot_ref[k, o * TOT + n : o * TOT + n + 1, :] = states[n][last : last + 1]
        excl_ref[o, STATE] = jnp.where(keep, pltpu.roll(span, shift, 0), 0.0)
        for k in range(copies):
            tot_ref[k, o * TOT + STATE : (o + 1) * TOT, :] = jnp.broadcast_to(
                span[last : last + 1], (TOT - STATE, LANES)
            )


def outputs_kernel(place_ref, rec_ref, dt_ref, excl_ref, tot_ref, decay_ref, y_ref, du_ref, coef_ref, sum_ref):
    steps = rec_ref.shape[0] // 8
    chunks = tot_ref.shape[0]
    place = place_ref[0]
    unpack(rec_ref, du_ref, coef_ref, dt_ref)
    for o in range(2):
        rates = decay_ref[o]
        entry = jnp.zeros((STATE, LANES), F32)
        for k in range(chunks) if o == 0 else range(chunks - 1, -1, -1):
            ahead = k < place if o == 0 else k > place
            base = o * TOT
            following = (
                jnp.exp2(rates * tot_ref[k, base + STATE : base + STATE + 1, :]) * entry
                + tot_ref[k, base : base + STATE, :]
            )
            entry = jnp.where(ahead, following, entry)
        decay = [jnp.broadcast_to(decay_ref[o, n : n + 1, :], (8, LANES)) for n in range(STATE)]
        states = tuple(
            jnp.exp2(decay[n] * excl_ref[o, STATE]) * entry[n : n + 1] + excl_ref[o, n]
            for n in range(STATE)
        )

        def advance(t, states):
            t = steps - 1 - t if o == 1 else t
            at = pl.ds(pl.multiple_of(t * 8, 8), 8)
            dt = dt_ref[o, at, :]
            du = du_ref[o, at, :]
            coef = coef_ref[at, :]
            new = []
            parts = []
            for n in range(STATE):
                lane = o * EACH + RANK + n
                b = jnp.broadcast_to(coef[:, lane : lane + 1], (8, LANES))
                c = jnp.broadcast_to(coef[:, lane + STATE : lane + STATE + 1], (8, LANES))
                h = jnp.exp2(decay[n] * dt) * states[n] + du * b
                new.append(h)
                parts.append(h * c)
            while len(parts) > 1:
                parts = [a + b for a, b in zip(parts[::2], parts[1::2])]
            if o == 0:
                sum_ref[at, :] = parts[0]
            else:
                sum_ref[at, :] = sum_ref[at, :] + parts[0]
            return tuple(new)

        lax.fori_loop(0, steps, advance, states, unroll=2)
    y_ref[...] = sum_ref[...].astype(BF16)


def final_kernel(yr_ref, yc_ref, act_ref, gate_ref, skip_ref, gain_ref, w_ref, live_ref, out_ref):
    turn = order_matrix(False)
    parts = []
    for k in range(8):
        first = jnp.dot(turn, yr_ref[k], preferred_element_type=F32)
        second = jnp.concatenate(
            [yc_ref[2 * k + h].astype(F32).reshape(8, 8, LANES) for h in range(2)], axis=1
        ).reshape(LANES, LANES)
        parts.append(first + second)
    combined = jnp.concatenate(join_slices(parts), axis=1)
    combined = combined + skip_ref[...] * act_ref[...].astype(F32)
    mean = jnp.mean(combined, axis=1, keepdims=True)
    centered = combined - mean
    variance = jnp.mean(centered * centered, axis=1, keepdims=True)
    normed = centered * lax.rsqrt(variance + 1e-05) * gain_ref[...]
    mixed = (normed * silu(gate_ref[...].astype(F32))).astype(BF16)
    out_ref[...] = (
        jnp.dot(mixed, w_ref[...], preferred_element_type=F32) * live_ref[...]
    ).astype(BF16)


def shifted(values, axis, step):
    count = lax.axis_size(axis)
    pairs = [(i, i + step) for i in range(count) if 0 <= i + step < count]
    return lax.ppermute(values, axis, pairs)


def padded_lanes(values, fill):
    pad = LANES - values.shape[-1]
    return jnp.pad(values, [(0, 0)] * (values.ndim - 1) + [(0, pad)], constant_values=fill)


def slice_params(dt_weight, dt_bias, decay_rate, first, piece):
    at = piece * SLICE
    dtw = lax.dynamic_slice_in_dim(dt_weight[first : first + 2], at, SLICE, 2)
    bias = lax.dynamic_slice_in_dim(dt_bias[first : first + 2], at, SLICE, 1)
    rates = lax.dynamic_slice_in_dim(decay_rate[first : first + 2], at, SLICE, 1)
    dtw = padded_lanes(dtw, 0)
    rows = jnp.zeros((2, LANES, LANES), BF16)
    for o in range(2):
        rows = lax.dynamic_update_slice(rows, dtw[o : o + 1], (o, o * EACH, 0))
    rows = rows.at[:, OFF_LANE, :].set(jnp.asarray(-1e30, BF16))
    bias = padded_lanes(bias, -1e30)[:, None, :]
    rates = padded_lanes(jnp.swapaxes(rates, 1, 2) * -LOG2E, 0)
    return rows, bias, rates


def per_device(
    patches, tissue, in_weight, conv_weight, conv_bias, x_weight, dt_weight, dt_bias,
    decay_rate, skip_gain, norm_gain, out_weight,
):
    tile_rows, tile_cols, channels = patches.shape
    inner = out_weight.shape[0]
    tokens = tile_rows * tile_cols
    row = lax.axis_index("row")
    col = lax.axis_index("col")
    top = shifted(patches[-1], "row", 1)
    bottom = shifted(patches[0], "row", -1)

    def edge(j):
        return jnp.concatenate([top[j : j + 1], patches[:, j], bottom[j : j + 1]], axis=0)

    left = shifted(edge(tile_cols - 1), "col", 1)
    right = shifted(edge(0), "col", -1)
    projected = jnp.dot(
        patches.reshape(tokens, channels), in_weight, preferred_element_type=F32
    ).astype(BF16)
    x_inner = projected[:, :inner]
    gate = projected[:, inner:]
    live = tissue.reshape(tokens, 1).astype(F32)
    half_width = x_weight.shape[1] // 2
    x_wide = jnp.concatenate(
        [padded_lanes(x_weight[:, :half_width], 0), padded_lanes(x_weight[:, half_width:], 0)], axis=1
    )
    params_r = slice_params(dt_weight, dt_bias, decay_rate, 0, col)
    params_c = slice_params(dt_weight, dt_bias, decay_rate, 2, row // 2)

    act, rec_r, rec_c = call(
        local_kernel,
        (
            jax.ShapeDtypeStruct((tokens, inner), BF16),
            jax.ShapeDtypeStruct((8, tokens, 2 * LANES), BF16),
            jax.ShapeDtypeStruct((16, tokens // 2, 2 * LANES), BF16),
        ),
        vmem(10),
        [pltpu.VMEM((10, 32, inner), F32)],
        name="local",
    )(
        x_inner, top, bottom, left, right, in_weight[:, :inner],
        conv_weight.reshape(9, inner), conv_bias.reshape(1, inner), x_wide, 1.0 - live,
    )

    length = 8 * tokens
    pair_scratch = [pltpu.VMEM((2, length, LANES), F32), pltpu.VMEM((length, LANES), F32)]

    def totals(rec, params, copies, name):
        return call(
            functools.partial(totals_kernel, copies),
            (
                jax.ShapeDtypeStruct((2, length, LANES), F32),
                jax.ShapeDtypeStruct((2, STATE + 1, 8, LANES), F32),
                jax.ShapeDtypeStruct((copies, 2 * TOT, LANES), F32),
            ),
            vmem(4),
            pair_scratch,
            flops=10**9,
            name=name,
        )(rec, *params)

    def outputs(place, rec, dt, excl, tot, rates, name):
        return call(
            outputs_kernel,
            jax.ShapeDtypeStruct((length, LANES), BF16),
            [pl.BlockSpec(memory_space=pltpu.SMEM)] + vmem(5),
            pair_scratch + [pltpu.VMEM((length, LANES), F32)],
            flops=10**9,
            name=name,
        )(place.reshape(1).astype(jnp.int32), rec, dt, excl, tot, rates)

    rec_r = lax.all_to_all(rec_r, "col", 0, 0).reshape(length, 2 * LANES)
    rec_c = lax.all_to_all(rec_c, "row", 0, 0).reshape(length, 2 * LANES)

    dt_r, excl_r, tot_r = totals(rec_r, params_r, 16, "totals_rows")
    dt_c, excl_c, tot_c = totals(rec_c, params_c, 1, "totals_cols")

    tot_r = lax.all_to_all(tot_r, "row", 0, 0)
    side = row % 2
    mate = lax.ppermute(tot_c, "row", [(i, i ^ 1) for i in range(16)])
    both = jnp.concatenate([jnp.where(side == 0, tot_c, mate), jnp.where(side == 0, mate, tot_c)])
    both = lax.all_to_all(jnp.broadcast_to(both[None], (8,) + both.shape), "col", 0, 0)
    tot_c = both.reshape(16, 2 * TOT, LANES)

    y_r = outputs(row, rec_r, dt_r, excl_r, tot_r, params_r[2], "outputs_rows")
    y_c = outputs(col * 2 + side, rec_c, dt_c, excl_c, tot_c, params_c[2], "outputs_cols")
    y_r = lax.all_to_all(y_r.reshape(8, tokens, LANES), "col", 0, 0)
    y_c = lax.all_to_all(y_c.reshape(16, tokens // 2, LANES), "row", 0, 0)

    result = call(
        final_kernel, jax.ShapeDtypeStruct((tokens, channels), BF16), vmem(8), name="final"
    )(
        y_r, y_c, act, gate, skip_gain.reshape(1, inner), norm_gain.reshape(1, inner), out_weight, live
    )
    return result.reshape(tile_rows, tile_cols, channels)


def solution(mesh):
    in_specs = (P("row", "col", None), P("row", "col")) + (P(),) * 10
    return jax.shard_map(
        per_device, mesh=mesh, in_specs=in_specs, out_specs=P("row", "col", None), check_vma=False
    )
```

```python
import functools
import math

import jax
import jax.numpy as jnp
from jax import lax
from jax.experimental import pallas as pl
from jax.experimental.pallas import tpu as pltpu
from jax.sharding import PartitionSpec as P

F32 = jnp.float32
BF16 = jnp.bfloat16
LANES = 128
SLICE = 96
STATE = 16
RANK = 24
EACH = RANK + 2 * STATE
OFF_LANE = 2 * EACH
TOT = 24
TURN = OFF_LANE
BLOCK = 16
LOG2E = math.log2(math.e)


def vmem(count):
    return [pl.BlockSpec(memory_space=pltpu.VMEM)] * count


def call(kernel, out_shape, in_specs, scratch=(), flops=10**7, name=None):
    return pl.pallas_call(
        kernel,
        out_shape=out_shape,
        in_specs=in_specs,
        out_specs=jax.tree.map(lambda _: pl.BlockSpec(memory_space=pltpu.VMEM), out_shape),
        scratch_shapes=list(scratch),
        compiler_params=pltpu.CompilerParams(vmem_limit_bytes=48 << 20),
        cost_estimate=pl.CostEstimate(flops=flops, bytes_accessed=4 * 10**6, transcendentals=0),
        name=name,
    )


def lane_iota(shape):
    return lax.broadcasted_iota(jnp.int32, shape, len(shape) - 1)


def softplus(x):
    return jnp.maximum(x, 0.0) + jnp.log1p(jnp.exp(-jnp.abs(x)))


def silu(x):
    return x * jax.nn.sigmoid(x)


def cut_slice(values, k):
    j0, off = divmod(SLICE * k, LANES)
    first = values[:, j0 * LANES : (j0 + 1) * LANES]
    if off == 0:
        return first
    shift = LANES - off
    head = pltpu.roll(first, shift, 1)
    if shift >= SLICE:
        return head
    second = values[:, (j0 + 1) * LANES : (j0 + 2) * LANES]
    tail = pltpu.roll(second, shift, 1)
    return jnp.where(lane_iota(head.shape) < shift, head, tail)


def join_slices(parts):
    tiles = []
    lane = lane_iota(parts[0].shape)
    for m in range(2):
        y0, y1, y2, y3 = parts[4 * m : 4 * m + 4]
        r1 = pltpu.roll(y1, 96, 1)
        r2 = pltpu.roll(y2, 64, 1)
        r3 = pltpu.roll(y3, 32, 1)
        tiles.append(jnp.where(lane < 96, y0, r1))
        tiles.append(jnp.where(lane < 64, r1, r2))
        tiles.append(jnp.where(lane < 32, r2, r3))
    return tiles


def order_matrix(to_columns):
    q = lax.broadcasted_iota(jnp.int32, (LANES, LANES), 0 if to_columns else 1)
    p = lax.broadcasted_iota(jnp.int32, (LANES, LANES), 1 if to_columns else 0)
    return (p == (q % 8) * 16 + q // 8).astype(F32).astype(BF16)


def local_kernel(
    place_ref, x_ref, top_ref, bottom_ref, left_ref, right_ref, w_ref, cw_ref, cb_ref, xw_ref, off_ref,
    *rest,
):
    act_ref, recr_refs, recc_ref = rest[0], rest[1:9], rest[9]
    frame_ref, xwide_ref, slices_ref = rest[10:]
    inner = x_ref.shape[1]
    weight = w_ref[:, :inner]

    def project(v):
        return jnp.dot(v, weight, preferred_element_type=F32).astype(BF16).astype(F32)

    frame_ref[1:9, 8:24, :] = x_ref[...].astype(F32).reshape(8, 16, inner)
    frame_ref[0:1, 8:24, :] = project(top_ref[...]).reshape(1, 16, inner)
    frame_ref[9:10, 8:24, :] = project(bottom_ref[...]).reshape(1, 16, inner)
    left = project(left_ref[...])
    right = project(right_ref[...])
    for i in range(10):
        frame_ref[i, 7:8, :] = left[i : i + 1]
        frame_ref[i, 24:25, :] = right[i : i + 1]
    total = jnp.zeros((8, 16, inner), F32) + cb_ref[...].reshape(1, 1, inner)
    for dc in range(3):
        for dr in range(3):
            k = dr * 3 + dc
            total = total + frame_ref[dr : dr + 8, 7 + dc : 23 + dc, :] * cw_ref[
                k : k + 1, :
            ].reshape(1, 1, inner)
    act = silu(total).reshape(LANES, inner).astype(BF16)
    act_ref[...] = act
    xwide_ref[:, LANES:] = jnp.zeros((inner, LANES), BF16)
    xwide_ref[:, : xw_ref.shape[1]] = xw_ref[...]
    coef = jnp.dot(act, xwide_ref[...], preferred_element_type=F32)
    lane = lane_iota((LANES, LANES))
    off = jnp.broadcast_to(off_ref[...], (LANES, LANES))
    coef_r = jnp.where(lane == OFF_LANE, off, jnp.where(lane < OFF_LANE, coef[:, :LANES], 0.0)).astype(BF16)
    coef_c = jnp.where(
        lane == (OFF_LANE + TURN) % LANES,
        off,
        jnp.where(lane >= TURN, coef[:, :LANES], coef[:, LANES:]),
    ).astype(BF16)
    turn = order_matrix(True)
    act_r = jnp.dot(turn, act, preferred_element_type=F32)
    coef_r = jnp.dot(turn, coef_r, preferred_element_type=F32).astype(BF16)
    wide = act.astype(F32)
    half = coef_c.astype(F32).reshape(8, 16, LANES)
    halves = [
        half[:, 8 * h : 8 * h + 8, :].reshape(64, LANES).astype(BF16) for h in range(2)
    ]
    for k in range(8):
        slices_ref[k] = cut_slice(act_r, k).astype(BF16)
        piece = cut_slice(wide, k).reshape(8, 16, LANES)
        for h in range(2):
            recc_ref[2 * k + h, :, :LANES] = (
                piece[:, 8 * h : 8 * h + 8, :].reshape(64, LANES).astype(BF16)
            )
            recc_ref[2 * k + h, :, LANES:] = halves[h]
    for j in range(8):
        recr_refs[j][:, :LANES] = slices_ref[(place_ref[0] + j) & 7]
        recr_refs[j][:, LANES:] = coef_r


def spread_matrix(spread_ref, turn, width):
    shape = (LANES, width * LANES)
    source = lax.broadcasted_iota(jnp.int32, shape, 0)
    tile = lax.broadcasted_iota(jnp.int32, shape, 1) // LANES
    for o in range(2):
        wanted = (tile + (o * EACH + RANK + turn)) & (LANES - 1)
        spread_ref[o] = (source == wanted).astype(F32).astype(BF16)


def drive(du_ref, dt_ref, act_ref):
    act = act_ref[...].astype(F32)
    for o in range(2):
        du_ref[o] = dt_ref[o] * act


def block_at(i, o, length):
    size = BLOCK * 8
    i = length // size - 1 - i if o == 1 else i
    return pl.multiple_of(i * size, size)


def totals_kernel(pieces, copies, first, turn, place_ref, *refs):
    recs, (dtw_ref, bias_ref, rates_ref) = refs[:pieces], refs[pieces : pieces + 3]
    dt_ref, act_ref, coef_ref, excl_ref, tot_ref, decay_ref = refs[pieces + 3 : pieces + 9]
    du_ref, rows_ref, spread_ref, bx_ref = refs[pieces + 9 :]
    length = act_ref.shape[0]
    step = length // pieces
    for j in range(pieces):
        at = pl.ds(pl.multiple_of(((place_ref[0] - j) & (pieces - 1)) * step, step), step)
        act_ref[at, :] = recs[j][:, :LANES]
        coef_ref[at, :] = recs[j][:, LANES:]
    inner = dtw_ref.shape[2]
    shift = jnp.where(place_ref[1] == 0, 0, inner - SLICE * place_ref[1])
    used = lane_iota((1, LANES)) < SLICE
    rows_ref[...] = jnp.zeros_like(rows_ref)
    coef = coef_ref[...]
    for o in range(2):
        dtw = pltpu.roll(dtw_ref[first + o].astype(F32), shift, 1)[:, :LANES]
        base = (o * EACH + turn) % LANES
        head = min(RANK, LANES - base)
        rows_ref[o, base : base + head, :] = dtw[:head]
        if head < RANK:
            rows_ref[o, : RANK - head, :] = dtw[head:]
        mark = (OFF_LANE + turn) % LANES
        rows_ref[o, mark : mark + 1, :] = jnp.full((1, LANES), -1e30, F32)
        bias = pltpu.roll(bias_ref[...], shift, 1)[first + o : first + o + 1, :LANES]
        bias = jnp.where(used, bias, -1e30)
        rates = pltpu.roll(rates_ref[first + o], shift, 1)[:, :LANES]
        decay_ref[o] = jnp.where(used, rates * -LOG2E, 0.0)
        z = jnp.dot(coef, rows_ref[o].astype(BF16), preferred_element_type=F32) + bias
        dt_ref[o] = softplus(z)
    drive(du_ref, dt_ref, act_ref)
    spread_matrix(spread_ref, turn, STATE)
    sub = lax.broadcasted_iota(jnp.int32, (8, LANES), 0)
    for o in range(2):
        decay = [jnp.broadcast_to(decay_ref[o, n : n + 1, :], (8, LANES)) for n in range(STATE)]

        def advance(i, carry):
            span, states = carry
            states = list(states)
            base = block_at(i, o, length)
            bx_ref[...] = jnp.dot(
                coef_ref[pl.ds(base, BLOCK * 8), :], spread_ref[o], preferred_element_type=F32
            )
            for t in range(BLOCK) if o == 0 else range(BLOCK - 1, -1, -1):
                dt = dt_ref[o, pl.ds(base + t * 8, 8), :]
                du = du_ref[o, pl.ds(base + t * 8, 8), :]
                for n in range(STATE):
                    b = bx_ref[t * 8 : t * 8 + 8, n * LANES : (n + 1) * LANES]
                    states[n] = jnp.exp2(decay[n] * dt) * states[n] + du * b
                span = span + dt
            return span, tuple(states)

        zero = jnp.zeros((8, LANES), F32)
        span, states = lax.fori_loop(0, length // (8 * BLOCK), advance, (zero, (zero,) * STATE))
        states = list(states)
        for k in (1, 2, 4):
            shift_k = k if o == 0 else 8 - k
            keep = sub >= k if o == 0 else sub < 8 - k
            for n in range(STATE):
                moved = jnp.where(keep, pltpu.roll(states[n], shift_k, 0), 0.0)
                states[n] = jnp.exp2(decay[n] * span) * moved + states[n]
            span = span + jnp.where(keep, pltpu.roll(span, shift_k, 0), 0.0)
        shift_k = 1 if o == 0 else 7
        keep = sub >= 1 if o == 0 else sub < 7
        last = 7 if o == 0 else 0
        for n in range(STATE):
            excl_ref[o, n] = jnp.where(keep, pltpu.roll(states[n], shift_k, 0), 0.0)
            for k in range(copies):
                tot_ref[k, o * TOT + n : o * TOT + n + 1, :] = states[n][last : last + 1]
        excl_ref[o, STATE] = jnp.where(keep, pltpu.roll(span, shift_k, 0), 0.0)
        for k in range(copies):
            tot_ref[k, o * TOT + STATE : (o + 1) * TOT, :] = jnp.broadcast_to(
                span[last : last + 1], (TOT - STATE, LANES)
            )


def outputs_kernel(pieces, parts_out, turn, place_ref, dt_ref, act_ref, coef_ref, excl_ref, decay_ref, *refs):
    tots, outs = refs[:pieces], refs[pieces : pieces + parts_out]
    du_ref, spread_ref, bx_ref, sum_ref, gathered_ref = refs[pieces + parts_out :]
    length = act_ref.shape[0]
    chunks = gathered_ref.shape[0]
    place = place_ref[2]
    per = chunks // pieces
    for j in range(pieces):
        at = pl.ds(((place_ref[0] - j) & (pieces - 1)) * per, per)
        gathered_ref[at] = tots[j][...]
    drive(du_ref, dt_ref, act_ref)
    spread_matrix(spread_ref, turn, 2 * STATE)
    for o in range(2):
        rates = decay_ref[o]
        entry = jnp.zeros((STATE, LANES), F32)
        for k in range(chunks) if o == 0 else range(chunks - 1, -1, -1):
            ahead = k < place if o == 0 else k > place
            base = o * TOT
            following = (
                jnp.exp2(rates * gathered_ref[k, base + STATE : base + STATE + 1, :]) * entry
                + gathered_ref[k, base : base + STATE, :]
            )
            entry = jnp.where(ahead, following, entry)
        decay = [jnp.broadcast_to(decay_ref[o, n : n + 1, :], (8, LANES)) for n in range(STATE)]
        states = tuple(
            jnp.exp2(decay[n] * excl_ref[o, STATE]) * entry[n : n + 1] + excl_ref[o, n]
            for n in range(STATE)
        )

        def advance(i, states):
            states = list(states)
            base = block_at(i, o, length)
            bx_ref[...] = jnp.dot(
                coef_ref[pl.ds(base, BLOCK * 8), :], spread_ref[o], preferred_element_type=F32
            )
            for t in range(BLOCK) if o == 0 else range(BLOCK - 1, -1, -1):
                at = pl.ds(base + t * 8, 8)
                dt = dt_ref[o, at, :]
                du = du_ref[o, at, :]
                parts = []
                for n in range(STATE):
                    b = bx_ref[t * 8 : t * 8 + 8, n * LANES : (n + 1) * LANES]
                    c = bx_ref[t * 8 : t * 8 + 8, (STATE + n) * LANES : (STATE + n + 1) * LANES]
                    states[n] = jnp.exp2(decay[n] * dt) * states[n] + du * b
                    parts.append(states[n] * c)
                while len(parts) > 1:
                    parts = [a + b for a, b in zip(parts[::2], parts[1::2])]
                if o == 0:
                    sum_ref[at, :] = parts[0]
                else:
                    sum_ref[at, :] = sum_ref[at, :] + parts[0]
            return tuple(states)

        lax.fori_loop(0, length // (8 * BLOCK), advance, states)
    if parts_out == 1:
        outs[0][...] = sum_ref[...].astype(BF16)
    else:
        step = length // parts_out
        for j in range(parts_out):
            at = pl.multiple_of(((place_ref[0] + j) & (parts_out - 1)) * step, step)
            outs[j][...] = sum_ref[pl.ds(at, step), :].astype(BF16)


def final_kernel(
    place_ref, yc_ref, act_ref, gate_ref, skip_ref, gain_ref, w_ref, live_ref, *refs
):
    yr_refs, out_ref, slices_ref = refs[:8], refs[8], refs[9]
    turn = order_matrix(False)
    for j in range(8):
        slices_ref[(place_ref[0] - j) & 7] = yr_refs[j][...]
    parts = []
    for k in range(8):
        first = jnp.dot(turn, slices_ref[k], preferred_element_type=F32)
        second = jnp.concatenate(
            [yc_ref[2 * k + h].astype(F32).reshape(8, 8, LANES) for h in range(2)], axis=1
        ).reshape(LANES, LANES)
        parts.append(first + second)
    combined = jnp.concatenate(join_slices(parts), axis=1)
    combined = combined + skip_ref[...] * act_ref[...].astype(F32)
    mean = jnp.mean(combined, axis=1, keepdims=True)
    centered = combined - mean
    variance = jnp.mean(centered * centered, axis=1, keepdims=True)
    normed = centered * lax.rsqrt(variance + 1e-05) * gain_ref[...]
    mixed = (normed * silu(gate_ref[...].astype(F32))).astype(BF16)
    out_ref[...] = (
        jnp.dot(mixed, w_ref[...], preferred_element_type=F32) * live_ref[...]
    ).astype(BF16)


def shifted(values, axis, step):
    count = lax.axis_size(axis)
    pairs = [(i, i + step) for i in range(count) if 0 <= i + step < count]
    return lax.ppermute(values, axis, pairs)


def around(values, axis):
    count = lax.axis_size(axis)
    return [
        v if j == 0 else lax.ppermute(v, axis, [(i, (i + j) % count) for i in range(count)])
        for j, v in enumerate(values)
    ]


def per_device(
    patches, tissue, in_weight, conv_weight, conv_bias, x_weight, dt_weight, dt_bias,
    decay_rate, skip_gain, norm_gain, out_weight,
):
    tile_rows, tile_cols, channels = patches.shape
    inner = out_weight.shape[0]
    tokens = tile_rows * tile_cols
    row = lax.axis_index("row").astype(jnp.int32)
    col = lax.axis_index("col").astype(jnp.int32)
    side = row % 2
    place_r = jnp.stack([col, col, row])
    place_c = jnp.stack([col, row // 2, col * 2 + side])
    top = shifted(patches[-1], "row", 1)
    bottom = shifted(patches[0], "row", -1)

    def edge(j):
        return jnp.concatenate([top[j : j + 1], patches[:, j], bottom[j : j + 1]], axis=0)

    left = shifted(edge(tile_cols - 1), "col", 1)
    right = shifted(edge(0), "col", -1)
    projected = jnp.dot(
        patches.reshape(tokens, channels), in_weight, preferred_element_type=F32
    ).astype(BF16)
    x_inner = projected[:, :inner]
    gate = projected[:, inner:]
    live = tissue.reshape(tokens, 1).astype(F32)
    rates = jnp.swapaxes(decay_rate, 1, 2)

    smem = [pl.BlockSpec(memory_space=pltpu.SMEM)]
    outs = call(
        local_kernel,
        (jax.ShapeDtypeStruct((tokens, inner), BF16),)
        + (jax.ShapeDtypeStruct((tokens, 2 * LANES), BF16),) * 8
        + (jax.ShapeDtypeStruct((16, tokens // 2, 2 * LANES), BF16),),
        smem + vmem(10),
        [
            pltpu.VMEM((10, 32, inner), F32),
            pltpu.VMEM((inner, 2 * LANES), BF16),
            pltpu.VMEM((8, tokens, LANES), BF16),
        ],
        name="local",
    )(
        place_r, x_inner, top, bottom, left, right, in_weight,
        conv_weight.reshape(9, inner), conv_bias.reshape(1, inner), x_weight, 1.0 - live,
    )
    act, rec_r, rec_c = outs[0], outs[1:9], outs[9]
    length = 8 * tokens
    wide = (length, LANES)

    def totals(place, recs, copies, first, turn, name):
        return call(
            functools.partial(totals_kernel, len(recs), copies, first, turn),
            (
                jax.ShapeDtypeStruct((2,) + wide, F32),
                jax.ShapeDtypeStruct(wide, BF16),
                jax.ShapeDtypeStruct(wide, BF16),
                jax.ShapeDtypeStruct((2, STATE + 1, 8, LANES), F32),
                jax.ShapeDtypeStruct((copies, 2 * TOT, LANES), F32),
                jax.ShapeDtypeStruct((2, STATE, LANES), F32),
            ),
            smem + vmem(len(recs) + 3),
            [
                pltpu.VMEM((2,) + wide, F32),
                pltpu.VMEM((2, LANES, LANES), F32),
                pltpu.VMEM((2, LANES, STATE * LANES), BF16),
                pltpu.VMEM((8 * BLOCK, STATE * LANES), F32),
            ],
            flops=10**9,
            name=name,
        )(place, *recs, dt_weight, dt_bias, rates)

    def outputs(place, dt, act, coef, excl, decay, tots, out, turn, name):
        pieces = len(tots)
        return call(
            functools.partial(outputs_kernel, pieces, len(out), turn),
            out,
            smem + vmem(pieces + 5),
            [
                pltpu.VMEM((2,) + wide, F32),
                pltpu.VMEM((2, LANES, 2 * STATE * LANES), BF16),
                pltpu.VMEM((8 * BLOCK, 2 * STATE * LANES), F32),
                pltpu.VMEM(wide, F32),
                pltpu.VMEM((16, 2 * TOT, LANES), F32),
            ],
            flops=10**9,
            name=name,
        )(place, dt, act, coef, excl, decay, *tots)

    rec_r = around(rec_r, "col")
    rec_c = lax.all_to_all(rec_c, "row", 0, 0).reshape(length, 2 * LANES)

    dt_r, act_r, coef_r, excl_r, tot_r, decay_r = totals(place_r, rec_r, 16, 0, 0, "totals_rows")
    dt_c, act_c, coef_c, excl_c, tot_c, decay_c = totals(place_c, [rec_c], 1, 2, TURN, "totals_cols")

    tot_r = lax.all_to_all(tot_r, "row", 0, 0)
    mate = lax.ppermute(tot_c, "row", [(i, i ^ 1) for i in range(16)])
    both = jnp.concatenate([jnp.where(side == 0, tot_c, mate), jnp.where(side == 0, mate, tot_c)])
    tot_c = around([both] * 8, "col")

    y_r = outputs(
        place_r, dt_r, act_r, coef_r, excl_r, decay_r, [tot_r],
        (jax.ShapeDtypeStruct((tokens, LANES), BF16),) * 8, 0, "outputs_rows",
    )
    (y_c,) = outputs(
        place_c, dt_c, act_c, coef_c, excl_c, decay_c, tot_c,
        (jax.ShapeDtypeStruct(wide, BF16),), TURN, "outputs_cols",
    )
    y_r = around(y_r, "col")
    y_c = lax.all_to_all(y_c.reshape(16, tokens // 2, LANES), "row", 0, 0)

    result = call(
        final_kernel,
        jax.ShapeDtypeStruct((tokens, channels), BF16),
        smem + vmem(15),
        [pltpu.VMEM((8, tokens, LANES), BF16)],
        name="final",
    )(
        place_r, y_c, act, gate, skip_gain.reshape(1, inner), norm_gain.reshape(1, inner),
        out_weight, live, *y_r,
    )
    return result.reshape(tile_rows, tile_cols, channels)


def solution(mesh):
    in_specs = (P("row", "col", None), P("row", "col")) + (P(),) * 10
    return jax.shard_map(
        per_device, mesh=mesh, in_specs=in_specs, out_specs=P("row", "col", None), check_vma=False
    )
```

```python
import functools
import math

import jax
import jax.numpy as jnp
from jax import lax
from jax.experimental import pallas as pl
from jax.experimental.pallas import tpu as pltpu
from jax.sharding import PartitionSpec as P

F32 = jnp.float32
BF16 = jnp.bfloat16
LANES = 128
SLICE = 96
STATE = 16
RANK = 24
EACH = RANK + 2 * STATE
OFF_LANE = 2 * EACH
TOT = 24
TURN = OFF_LANE
BLOCK = 32
LOG2E = math.log2(math.e)


def vmem(count):
    return [pl.BlockSpec(memory_space=pltpu.VMEM)] * count


def call(kernel, out_shape, in_specs, scratch=(), flops=10**7, grant=16, name=None):
    return pl.pallas_call(
        kernel,
        out_shape=out_shape,
        in_specs=in_specs,
        out_specs=jax.tree.map(lambda _: pl.BlockSpec(memory_space=pltpu.VMEM), out_shape),
        scratch_shapes=list(scratch),
        compiler_params=pltpu.CompilerParams(vmem_limit_bytes=grant << 20),
        cost_estimate=pl.CostEstimate(flops=flops, bytes_accessed=4 * 10**6, transcendentals=0),
        name=name,
    )


def lane_iota(shape):
    return lax.broadcasted_iota(jnp.int32, shape, len(shape) - 1)


def softplus(x):
    return jnp.maximum(x, 0.0) + jnp.log1p(jnp.exp(-jnp.abs(x)))


def silu(x):
    return x * jax.nn.sigmoid(x)


def cut_slice(values, k):
    j0, off = divmod(SLICE * k, LANES)
    first = values[:, j0 * LANES : (j0 + 1) * LANES]
    if off == 0:
        return first
    shift = LANES - off
    head = pltpu.roll(first, shift, 1)
    if shift >= SLICE:
        return head
    second = values[:, (j0 + 1) * LANES : (j0 + 2) * LANES]
    tail = pltpu.roll(second, shift, 1)
    return jnp.where(lane_iota(head.shape) < shift, head, tail)


def join_slices(parts):
    tiles = []
    lane = lane_iota(parts[0].shape)
    for m in range(2):
        y0, y1, y2, y3 = parts[4 * m : 4 * m + 4]
        r1 = pltpu.roll(y1, 96, 1)
        r2 = pltpu.roll(y2, 64, 1)
        r3 = pltpu.roll(y3, 32, 1)
        tiles.append(jnp.where(lane < 96, y0, r1))
        tiles.append(jnp.where(lane < 64, r1, r2))
        tiles.append(jnp.where(lane < 32, r2, r3))
    return tiles


def order_matrix(to_columns):
    q = lax.broadcasted_iota(jnp.int32, (LANES, LANES), 0 if to_columns else 1)
    p = lax.broadcasted_iota(jnp.int32, (LANES, LANES), 1 if to_columns else 0)
    return (p == (q % 8) * 16 + q // 8).astype(F32).astype(BF16)


def local_kernel(
    place_ref, x_ref, top_ref, bottom_ref, left_ref, right_ref, w_ref, cw_ref, cb_ref, xw_ref, off_ref,
    *rest,
):
    act_ref, recr_refs, recc_ref = rest[0], rest[1:9], rest[9]
    frame_ref, xwide_ref, slices_ref = rest[10:]
    inner = x_ref.shape[1]
    weight = w_ref[:, :inner]

    def project(v):
        return jnp.dot(v, weight, preferred_element_type=F32).astype(BF16).astype(F32)

    frame_ref[1:9, 8:24, :] = x_ref[...].astype(F32).reshape(8, 16, inner)
    frame_ref[0:1, 8:24, :] = project(top_ref[...]).reshape(1, 16, inner)
    frame_ref[9:10, 8:24, :] = project(bottom_ref[...]).reshape(1, 16, inner)
    left = project(left_ref[...])
    right = project(right_ref[...])
    for i in range(10):
        frame_ref[i, 7:8, :] = left[i : i + 1]
        frame_ref[i, 24:25, :] = right[i : i + 1]
    total = jnp.zeros((8, 16, inner), F32) + cb_ref[...].reshape(1, 1, inner)
    for dc in range(3):
        for dr in range(3):
            k = dr * 3 + dc
            total = total + frame_ref[dr : dr + 8, 7 + dc : 23 + dc, :] * cw_ref[
                k : k + 1, :
            ].reshape(1, 1, inner)
    act = silu(total).reshape(LANES, inner).astype(BF16)
    act_ref[...] = act
    xwide_ref[:, LANES:] = jnp.zeros((inner, LANES), BF16)
    xwide_ref[:, : xw_ref.shape[1]] = xw_ref[...]
    coef = jnp.dot(act, xwide_ref[...], preferred_element_type=F32)
    lane = lane_iota((LANES, LANES))
    off = jnp.broadcast_to(off_ref[...], (LANES, LANES))
    coef_r = jnp.where(lane == OFF_LANE, off, jnp.where(lane < OFF_LANE, coef[:, :LANES], 0.0)).astype(BF16)
    coef_c = jnp.where(
        lane == (OFF_LANE + TURN) % LANES,
        off,
        jnp.where(lane >= TURN, coef[:, :LANES], coef[:, LANES:]),
    ).astype(BF16)
    turn = order_matrix(True)
    act_r = jnp.dot(turn, act, preferred_element_type=F32)
    coef_r = jnp.dot(turn, coef_r, preferred_element_type=F32).astype(BF16)
    wide = act.astype(F32)
    half = coef_c.astype(F32).reshape(8, 16, LANES)
    halves = [
        half[:, 8 * h : 8 * h + 8, :].reshape(64, LANES).astype(BF16) for h in range(2)
    ]
    for k in range(8):
        slices_ref[k] = cut_slice(act_r, k).astype(BF16)
        piece = cut_slice(wide, k).reshape(8, 16, LANES)
        for h in range(2):
            recc_ref[2 * k + h, :, :LANES] = (
                piece[:, 8 * h : 8 * h + 8, :].reshape(64, LANES).astype(BF16)
            )
            recc_ref[2 * k + h, :, LANES:] = halves[h]
    for j in range(8):
        recr_refs[j][:, :LANES] = slices_ref[(place_ref[0] + j) & 7]
        recr_refs[j][:, LANES:] = coef_r


def spread_matrix(spread_ref, turn, width):
    shape = (LANES, width * LANES)
    source = lax.broadcasted_iota(jnp.int32, shape, 0)
    tile = lax.broadcasted_iota(jnp.int32, shape, 1) // LANES
    for o in range(2):
        wanted = (tile + (o * EACH + RANK + turn)) & (LANES - 1)
        spread_ref[o] = (source == wanted).astype(F32).astype(BF16)


def prepare(recs, place, rows_ref, bias, dt_ref, du_ref, coef_ref):
    length = coef_ref.shape[0]
    size = length // 8
    for j in range(8):
        if len(recs) == 1:
            rec = recs[0].at[j * size : (j + 1) * size]
            at = pl.ds(j * size, size)
        else:
            rec = recs[j]
            at = pl.ds(pl.multiple_of(((place - j) & 7) * size, size), size)
        coef = rec[:, LANES:]
        act = rec[:, :LANES].astype(F32)
        coef_ref[at, :] = coef
        for o in range(2):
            dt = softplus(jnp.dot(coef, rows_ref[o], preferred_element_type=F32) + bias[o])
            dt_ref[o, at, :] = dt
            du_ref[o, at, :] = dt * act


def block_at(i, o, length):
    size = BLOCK * 8
    i = length // size - 1 - i if o == 1 else i
    return pl.multiple_of(i * size, size)


def totals_kernel(pieces, copies, first, turn, place_ref, *refs):
    recs, (dtw_ref, bias_ref, rates_ref) = refs[:pieces], refs[pieces : pieces + 3]
    excl_ref, tot_ref, decay_ref, rows_ref = refs[pieces + 3 : pieces + 7]
    dt_ref, du_ref, coef_ref, wide_ref, spread_ref, bx_ref = refs[pieces + 7 :]
    length = coef_ref.shape[0]
    inner = dtw_ref.shape[2]
    shift = jnp.where(place_ref[1] == 0, 0, inner - SLICE * place_ref[1])
    used = lane_iota((1, LANES)) < SLICE
    wide_ref[...] = jnp.zeros_like(wide_ref)
    for o in range(2):
        dtw = pltpu.roll(dtw_ref[first + o].astype(F32), shift, 1)[:, :LANES]
        base = (o * EACH + turn) % LANES
        head = min(RANK, LANES - base)
        wide_ref[o, base : base + head, :] = dtw[:head]
        if head < RANK:
            wide_ref[o, : RANK - head, :] = dtw[head:]
        mark = (OFF_LANE + turn) % LANES
        wide_ref[o, mark : mark + 1, :] = jnp.full((1, LANES), -1e30, F32)
        rows_ref[o] = wide_ref[o].astype(BF16)
        bias = pltpu.roll(bias_ref[...], shift, 1)[first + o : first + o + 1, :LANES]
        rates = pltpu.roll(rates_ref[first + o], shift, 1)[:, :LANES]
        decay_ref[o, :STATE] = jnp.where(used, rates * -LOG2E, 0.0)
        decay_ref[o, STATE:] = jnp.broadcast_to(jnp.where(used, bias, -1e30), (TOT - STATE, LANES))
    bias = [decay_ref[o, STATE : STATE + 1, :] for o in range(2)]
    prepare(recs, place_ref[0], rows_ref, bias, dt_ref, du_ref, coef_ref)
    spread_matrix(spread_ref, turn, STATE)
    sub = lax.broadcasted_iota(jnp.int32, (8, LANES), 0)
    for o in range(2):
        decay = [jnp.broadcast_to(decay_ref[o, n : n + 1, :], (8, LANES)) for n in range(STATE)]

        def advance(i, carry):
            span, states = carry
            states = list(states)
            base = block_at(i, o, length)
            bx_ref[...] = jnp.dot(
                coef_ref[pl.ds(base, BLOCK * 8), :], spread_ref[o], preferred_element_type=F32
            )
            for t in range(BLOCK) if o == 0 else range(BLOCK - 1, -1, -1):
                dt = dt_ref[o, pl.ds(base + t * 8, 8), :]
                du = du_ref[o, pl.ds(base + t * 8, 8), :]
                for n in range(STATE):
                    b = bx_ref[t * 8 : t * 8 + 8, n * LANES : (n + 1) * LANES]
                    states[n] = jnp.exp2(decay[n] * dt) * states[n] + du * b
                span = span + dt
            return span, tuple(states)

        zero = jnp.zeros((8, LANES), F32)
        span, states = lax.fori_loop(0, length // (8 * BLOCK), advance, (zero, (zero,) * STATE))
        states = list(states)
        for k in (1, 2, 4):
            shift_k = k if o == 0 else 8 - k
            keep = sub >= k if o == 0 else sub < 8 - k
            for n in range(STATE):
                moved = jnp.where(keep, pltpu.roll(states[n], shift_k, 0), 0.0)
                states[n] = jnp.exp2(decay[n] * span) * moved + states[n]
            span = span + jnp.where(keep, pltpu.roll(span, shift_k, 0), 0.0)
        shift_k = 1 if o == 0 else 7
        keep = sub >= 1 if o == 0 else sub < 7
        last = 7 if o == 0 else 0
        for n in range(STATE):
            excl_ref[o, n] = jnp.where(keep, pltpu.roll(states[n], shift_k, 0), 0.0)
            for k in range(copies):
                tot_ref[k, o * TOT + n : o * TOT + n + 1, :] = states[n][last : last + 1]
        excl_ref[o, STATE] = jnp.where(keep, pltpu.roll(span, shift_k, 0), 0.0)
        for k in range(copies):
            tot_ref[k, o * TOT + STATE : (o + 1) * TOT, :] = jnp.broadcast_to(
                span[last : last + 1], (TOT - STATE, LANES)
            )


def outputs_kernel(pieces, parts_out, turn, place_ref, gathered_ref, excl_ref, decay_ref, rows_ref, *refs):
    recs, outs = refs[:pieces], refs[pieces : pieces + parts_out]
    dt_ref, du_ref, coef_ref, spread_ref, bx_ref, sum_ref = refs[pieces + parts_out :]
    length = coef_ref.shape[0]
    chunks = gathered_ref.shape[0]
    bias = [decay_ref[o, STATE : STATE + 1, :] for o in range(2)]
    prepare(recs, place_ref[0], rows_ref, bias, dt_ref, du_ref, coef_ref)
    place = place_ref[2]
    spread_matrix(spread_ref, turn, 2 * STATE)
    for o in range(2):
        rates = decay_ref[o, :STATE]
        entry = jnp.zeros((STATE, LANES), F32)
        for k in range(chunks) if o == 0 else range(chunks - 1, -1, -1):
            ahead = k < place if o == 0 else k > place
            base = o * TOT
            following = (
                jnp.exp2(rates * gathered_ref[k, base + STATE : base + STATE + 1, :]) * entry
                + gathered_ref[k, base : base + STATE, :]
            )
            entry = jnp.where(ahead, following, entry)
        decay = [jnp.broadcast_to(decay_ref[o, n : n + 1, :], (8, LANES)) for n in range(STATE)]
        states = tuple(
            jnp.exp2(decay[n] * excl_ref[o, STATE]) * entry[n : n + 1] + excl_ref[o, n]
            for n in range(STATE)
        )

        def advance(i, states):
            states = list(states)
            base = block_at(i, o, length)
            bx_ref[...] = jnp.dot(
                coef_ref[pl.ds(base, BLOCK * 8), :], spread_ref[o], preferred_element_type=F32
            )
            for t in range(BLOCK) if o == 0 else range(BLOCK - 1, -1, -1):
                at = pl.ds(base + t * 8, 8)
                dt = dt_ref[o, at, :]
                du = du_ref[o, at, :]
                parts = []
                for n in range(STATE):
                    b = bx_ref[t * 8 : t * 8 + 8, n * LANES : (n + 1) * LANES]
                    c = bx_ref[t * 8 : t * 8 + 8, (STATE + n) * LANES : (STATE + n + 1) * LANES]
                    states[n] = jnp.exp2(decay[n] * dt) * states[n] + du * b
                    parts.append(states[n] * c)
                while len(parts) > 1:
                    parts = [a + b for a, b in zip(parts[::2], parts[1::2])]
                if o == 0:
                    sum_ref[at, :] = parts[0]
                else:
                    sum_ref[at, :] = sum_ref[at, :] + parts[0]
            return tuple(states)

        lax.fori_loop(0, length // (8 * BLOCK), advance, states)
    if parts_out == 1:
        outs[0][...] = sum_ref[...].astype(BF16)
    else:
        step = length // parts_out
        for j in range(parts_out):
            at = pl.multiple_of(((place_ref[0] + j) & (parts_out - 1)) * step, step)
            outs[j][...] = sum_ref[pl.ds(at, step), :].astype(BF16)


def final_kernel(
    place_ref, yc_ref, act_ref, gate_ref, skip_ref, gain_ref, w_ref, live_ref, *refs
):
    yr_refs, out_ref, slices_ref = refs[:8], refs[8], refs[9]
    turn = order_matrix(False)
    for j in range(8):
        slices_ref[(place_ref[0] - j) & 7] = yr_refs[j][...]
    parts = []
    for k in range(8):
        first = jnp.dot(turn, slices_ref[k], preferred_element_type=F32)
        second = jnp.concatenate(
            [yc_ref[2 * k + h].astype(F32).reshape(8, 8, LANES) for h in range(2)], axis=1
        ).reshape(LANES, LANES)
        parts.append(first + second)
    combined = jnp.concatenate(join_slices(parts), axis=1)
    combined = combined + skip_ref[...] * act_ref[...].astype(F32)
    mean = jnp.mean(combined, axis=1, keepdims=True)
    centered = combined - mean
    variance = jnp.mean(centered * centered, axis=1, keepdims=True)
    normed = centered * lax.rsqrt(variance + 1e-05) * gain_ref[...]
    mixed = (normed * silu(gate_ref[...].astype(F32))).astype(BF16)
    out_ref[...] = (
        jnp.dot(mixed, w_ref[...], preferred_element_type=F32) * live_ref[...]
    ).astype(BF16)


def shifted(values, axis, step):
    count = lax.axis_size(axis)
    pairs = [(i, i + step) for i in range(count) if 0 <= i + step < count]
    return lax.ppermute(values, axis, pairs)


def around(values, axis):
    count = lax.axis_size(axis)
    return [
        v if j == 0 else lax.ppermute(v, axis, [(i, (i + j) % count) for i in range(count)])
        for j, v in enumerate(values)
    ]


def per_device(
    patches, tissue, in_weight, conv_weight, conv_bias, x_weight, dt_weight, dt_bias,
    decay_rate, skip_gain, norm_gain, out_weight,
):
    tile_rows, tile_cols, channels = patches.shape
    inner = out_weight.shape[0]
    tokens = tile_rows * tile_cols
    row = lax.axis_index("row").astype(jnp.int32)
    col = lax.axis_index("col").astype(jnp.int32)
    side = row % 2
    place_r = jnp.stack([col, col, row])
    place_c = jnp.stack([col, row // 2, col * 2 + side])
    top = shifted(patches[-1], "row", 1)
    bottom = shifted(patches[0], "row", -1)

    def edge(j):
        return jnp.concatenate([top[j : j + 1], patches[:, j], bottom[j : j + 1]], axis=0)

    left = shifted(edge(tile_cols - 1), "col", 1)
    right = shifted(edge(0), "col", -1)
    projected = jnp.dot(
        patches.reshape(tokens, channels), in_weight, preferred_element_type=F32
    ).astype(BF16)
    x_inner = projected[:, :inner]
    gate = projected[:, inner:]
    live = tissue.reshape(tokens, 1).astype(F32)
    rates = jnp.swapaxes(decay_rate, 1, 2)

    smem = [pl.BlockSpec(memory_space=pltpu.SMEM)]
    outs = call(
        local_kernel,
        (jax.ShapeDtypeStruct((tokens, inner), BF16),)
        + (jax.ShapeDtypeStruct((tokens, 2 * LANES), BF16),) * 8
        + (jax.ShapeDtypeStruct((16, tokens // 2, 2 * LANES), BF16),),
        smem + vmem(10),
        [
            pltpu.VMEM((10, 32, inner), F32),
            pltpu.VMEM((inner, 2 * LANES), BF16),
            pltpu.VMEM((8, tokens, LANES), BF16),
        ],
        name="local",
    )(
        place_r, x_inner, top, bottom, left, right, in_weight,
        conv_weight.reshape(9, inner), conv_bias.reshape(1, inner), x_weight, 1.0 - live,
    )
    act, rec_r, rec_c = outs[0], outs[1:9], outs[9]
    length = 8 * tokens
    wide = (length, LANES)

    scratch = [
        pltpu.VMEM((2,) + wide, F32),
        pltpu.VMEM((2,) + wide, F32),
        pltpu.VMEM(wide, BF16),
    ]

    def totals(place, recs, copies, first, turn, name):
        return call(
            functools.partial(totals_kernel, len(recs), copies, first, turn),
            (
                jax.ShapeDtypeStruct((2, STATE + 1, 8, LANES), F32),
                jax.ShapeDtypeStruct((copies, 2 * TOT, LANES), F32),
                jax.ShapeDtypeStruct((2, TOT, LANES), F32),
                jax.ShapeDtypeStruct((2, LANES, LANES), BF16),
            ),
            smem + vmem(len(recs) + 3),
            scratch
            + [
                pltpu.VMEM((2, LANES, LANES), F32),
                pltpu.VMEM((2, LANES, STATE * LANES), BF16),
                pltpu.VMEM((8 * BLOCK, STATE * LANES), F32),
            ],
            flops=10**9,
            grant=20,
            name=name,
        )(place, *recs, dt_weight, dt_bias, rates)

    def outputs(place, tot, excl, decay, rows, recs, out, turn, name):
        return call(
            functools.partial(outputs_kernel, len(recs), len(out), turn),
            out,
            smem + vmem(len(recs) + 4),
            scratch
            + [
                pltpu.VMEM((2, LANES, 2 * STATE * LANES), BF16),
                pltpu.VMEM((8 * BLOCK, 2 * STATE * LANES), F32),
                pltpu.VMEM(wide, F32),
            ],
            flops=10**9,
            grant=24,
            name=name,
        )(place, tot, excl, decay, rows, *recs)

    rec_r = around(rec_r, "col")
    rec_c = lax.all_to_all(rec_c, "row", 0, 0).reshape(length, 2 * LANES)

    excl_r, tot_r, decay_r, rows_r = totals(place_r, rec_r, 16, 0, 0, "totals_rows")
    excl_c, tot_c, decay_c, rows_c = totals(place_c, [rec_c], 1, 2, TURN, "totals_cols")

    tot_r = lax.all_to_all(tot_r, "row", 0, 0)
    mate = lax.ppermute(tot_c, "row", [(i, i ^ 1) for i in range(16)])
    both = jnp.concatenate([jnp.where(side == 0, tot_c, mate), jnp.where(side == 0, mate, tot_c)])
    tot_c = lax.all_to_all(jnp.broadcast_to(both[None], (8,) + both.shape), "col", 0, 0)
    tot_c = tot_c.reshape(16, 2 * TOT, LANES)

    y_r = outputs(
        place_r, tot_r, excl_r, decay_r, rows_r, rec_r,
        (jax.ShapeDtypeStruct((tokens, LANES), BF16),) * 8, 0, "outputs_rows",
    )
    (y_c,) = outputs(
        place_c, tot_c, excl_c, decay_c, rows_c, [rec_c],
        (jax.ShapeDtypeStruct(wide, BF16),), TURN, "outputs_cols",
    )
    y_c, *y_r = lax.optimization_barrier((y_c, *y_r))
    y_r = around(y_r, "col")
    y_c = lax.all_to_all(y_c.reshape(16, tokens // 2, LANES), "row", 0, 0)

    result = call(
        final_kernel,
        jax.ShapeDtypeStruct((tokens, channels), BF16),
        smem + vmem(15),
        [pltpu.VMEM((8, tokens, LANES), BF16)],
        name="final",
    )(
        place_r, y_c, act, gate, skip_gain.reshape(1, inner), norm_gain.reshape(1, inner),
        out_weight, live, *y_r,
    )
    return result.reshape(tile_rows, tile_cols, channels)


def solution(mesh):
    in_specs = (P("row", "col", None), P("row", "col")) + (P(),) * 10
    return jax.shard_map(
        per_device, mesh=mesh, in_specs=in_specs, out_specs=P("row", "col", None), check_vma=False
    )
```

```python
import functools
import math

import jax
import jax.numpy as jnp
from jax import lax
from jax.experimental import pallas as pl
from jax.experimental.pallas import tpu as pltpu
from jax.sharding import PartitionSpec as P

F32 = jnp.float32
BF16 = jnp.bfloat16
LANES = 128
SLICE = 96
STATE = 16
RANK = 24
EACH = RANK + 2 * STATE
OFF_LANE = 2 * EACH
TOT = 24
BLOCK = 64
LOG2E = math.log2(math.e)
HALF = 64


def vmem(count):
    return [pl.BlockSpec(memory_space=pltpu.VMEM)] * count


def call(kernel, out_shape, in_specs, scratch=(), flops=10**7, grant=16, name=None):
    return pl.pallas_call(
        kernel,
        out_shape=out_shape,
        in_specs=in_specs,
        out_specs=jax.tree.map(lambda _: pl.BlockSpec(memory_space=pltpu.VMEM), out_shape),
        scratch_shapes=list(scratch),
        compiler_params=pltpu.CompilerParams(vmem_limit_bytes=grant << 20),
        cost_estimate=pl.CostEstimate(flops=flops, bytes_accessed=4 * 10**6, transcendentals=0),
        name=name,
    )


def lane_iota(shape):
    return lax.broadcasted_iota(jnp.int32, shape, len(shape) - 1)


def softplus(x):
    u = jnp.exp2(jnp.abs(x) * -LOG2E)
    series = u * (1.0 - u * (0.5 - u * (1.0 / 3.0 - u * 0.25)))
    return jnp.maximum(x, 0.0) + jnp.where(u < 0.03, series, jnp.log(1.0 + u))


def silu(x):
    return x * jax.nn.sigmoid(x)


def cut_slice(values, k):
    j0, off = divmod(SLICE * k, LANES)
    first = values[:, j0 * LANES : (j0 + 1) * LANES]
    if off == 0:
        return first
    shift = LANES - off
    head = pltpu.roll(first, shift, 1)
    if shift >= SLICE:
        return head
    second = values[:, (j0 + 1) * LANES : (j0 + 2) * LANES]
    tail = pltpu.roll(second, shift, 1)
    return jnp.where(lane_iota(head.shape) < shift, head, tail)


def join_slices(parts):
    tiles = []
    lane = lane_iota(parts[0].shape)
    for m in range(2):
        y0, y1, y2, y3 = parts[4 * m : 4 * m + 4]
        r1 = pltpu.roll(y1, 96, 1)
        r2 = pltpu.roll(y2, 64, 1)
        r3 = pltpu.roll(y3, 32, 1)
        tiles.append(jnp.where(lane < 96, y0, r1))
        tiles.append(jnp.where(lane < 64, r1, r2))
        tiles.append(jnp.where(lane < 32, r2, r3))
    return tiles


def cut_narrow(values, k, start):
    j0, off = divmod(SLICE // 2 * k, LANES)
    shift = (start - off) % LANES
    first = values[:, j0 * LANES : (j0 + 1) * LANES]
    head = first if shift == 0 else pltpu.roll(first, shift, 1)
    if off + SLICE // 2 <= LANES:
        return head
    second = values[:, (j0 + 1) * LANES : (j0 + 2) * LANES]
    tail = pltpu.roll(second, shift, 1)
    return jnp.where(lane_iota(head.shape) < start + LANES - off, head, tail)


def join_narrow(parts, start):
    lane = lane_iota(parts[0].shape)

    def pick(chosen, bounds):
        out = chosen[-1]
        for value, bound in zip(chosen[-2::-1], bounds[::-1]):
            out = jnp.where(lane < bound, value, out)
        return out

    tiles = []
    for m in range(2):
        r = []
        for k in range(8):
            shift = (48 * k - start) % LANES
            y = parts[8 * m + k]
            r.append(y if shift == 0 else pltpu.roll(y, shift, 1))
        tiles.append(pick(r[0:3], (48, 96)))
        tiles.append(pick(r[2:6], (16, 64, 112)))
        tiles.append(pick(r[5:8], (32, 80)))
    return tiles


def order_matrix(to_columns):
    q = lax.broadcasted_iota(jnp.int32, (LANES, LANES), 0 if to_columns else 1)
    p = lax.broadcasted_iota(jnp.int32, (LANES, LANES), 1 if to_columns else 0)
    return (p == (q % 8) * 16 + q // 8).astype(F32).astype(BF16)


def column(col, chips, flip):
    return ((col + 2 * chips) & 7) ^ flip


def merge_kernel(near_ref, far_ref, *out_refs):
    for j, out_ref in enumerate(out_refs):
        out_ref[0] = near_ref[j]
        out_ref[1] = far_ref[j]


def local_kernel(
    place_ref, x_ref, top_ref, bottom_ref, left_ref, right_ref, w_ref, cw_ref, cb_ref, xw_ref, off_ref,
    *rest,
):
    act_ref, near_ref, far_ref, recc_ref, frame_ref, xwide_ref, slices_ref = rest
    inner = x_ref.shape[1]
    weight = w_ref[:, :inner]

    def project(v):
        return jnp.dot(v, weight, preferred_element_type=F32).astype(BF16).astype(F32)

    frame_ref[1:9, 8:24, :] = x_ref[...].astype(F32).reshape(8, 16, inner)
    frame_ref[0:1, 8:24, :] = project(top_ref[...]).reshape(1, 16, inner)
    frame_ref[9:10, 8:24, :] = project(bottom_ref[...]).reshape(1, 16, inner)
    left = project(left_ref[...])
    right = project(right_ref[...])
    for i in range(10):
        frame_ref[i, 7:8, :] = left[i : i + 1]
        frame_ref[i, 24:25, :] = right[i : i + 1]
    total = jnp.zeros((8, 16, inner), F32) + cb_ref[...].reshape(1, 1, inner)
    for dc in range(3):
        for dr in range(3):
            k = dr * 3 + dc
            total = total + frame_ref[dr : dr + 8, 7 + dc : 23 + dc, :] * cw_ref[
                k : k + 1, :
            ].reshape(1, 1, inner)
    act = silu(total).reshape(LANES, inner).astype(BF16)
    act_ref[...] = act
    xwide_ref[:, LANES:] = jnp.zeros((inner, LANES), BF16)
    xwide_ref[:, : xw_ref.shape[1]] = xw_ref[...]
    coef = jnp.dot(act, xwide_ref[...], preferred_element_type=F32)
    lane = lane_iota((LANES, LANES))
    off = jnp.broadcast_to(off_ref[...], (LANES, LANES))
    coef_r = jnp.where(lane == OFF_LANE, off, jnp.where(lane < OFF_LANE, coef[:, :LANES], 0.0)).astype(BF16)
    coef_c = pltpu.roll(jnp.where(lane >= OFF_LANE, coef[:, :LANES], coef[:, LANES:]), 16, 1)
    coef_c = jnp.where(lane == OFF_LANE, off, jnp.where(lane < OFF_LANE, coef_c, 0.0))
    turn = order_matrix(True)
    act_r = jnp.dot(turn, act, preferred_element_type=F32)
    coef_r = jnp.dot(turn, coef_r, preferred_element_type=F32).astype(BF16)
    wide = act.astype(F32).reshape(8, 16, inner)
    half = coef_c.reshape(8, 16, LANES)
    sides = [wide[:, 8 * h : 8 * h + 8, :].reshape(HALF, inner) for h in range(2)]
    coefs = [half[:, 8 * h : 8 * h + 8, :].reshape(HALF, LANES).astype(BF16) for h in range(2)]
    for k in range(8):
        slices_ref[k] = cut_slice(act_r, k).astype(BF16)
    for k in range(16):
        pair = [cut_narrow(sides[h], k, HALF * h) for h in range(2)]
        recc_ref[k, :, :LANES] = jnp.where(
            lane_iota(pair[0].shape) < HALF, pair[0], pair[1]
        ).astype(BF16)
        for h in range(2):
            recc_ref[k, :, (1 + h) * LANES : (2 + h) * LANES] = coefs[h]
    for ref, flip in ((near_ref, 0), (far_ref, 1)):
        for j in range(4):
            ref[j, :, :LANES] = slices_ref[column(place_ref[0], j, flip)]
            ref[j, :, LANES:] = coef_r


def spread_matrix(spread_ref):
    halves = spread_ref.shape[0] // LANES
    low, high = 16, 64
    spread_ref[...] = jnp.zeros_like(spread_ref)
    shape = (high - low, spread_ref.shape[1])
    source = lax.broadcasted_iota(jnp.int32, shape, 0) + low
    place = lax.broadcasted_iota(jnp.int32, shape, 1)
    hit = source == RANK + place // LANES
    for h in range(halves):
        side = hit if halves == 1 else jnp.logical_and(hit, ((place // HALF) & 1) == h)
        spread_ref[h * LANES + low : h * LANES + high, :] = side.astype(F32).astype(BF16)


def prepare(recs, place, rows_ref, bias, dt_ref, du_ref, coef_ref):
    length = dt_ref.shape[1]
    halves = coef_ref.shape[2] // LANES
    size = length // 8
    for j in range(8):
        if len(recs) == 1:
            rec = recs[0].at[j * size : (j + 1) * size]
            at = pl.ds(j * size, size)
        else:
            rec = recs[j // 2].at[j % 2]
            at = pl.ds(pl.multiple_of(column(place, -(j // 2), j % 2) * size, size), size)
        act = rec[:, :LANES].astype(F32)
        for o in range(2):
            z = bias[o]
            for h in range(halves):
                coef = rec[:, (1 + h) * LANES : (2 + h) * LANES]
                if o == 1:
                    coef = pltpu.roll(coef.astype(F32), LANES - EACH, 1).astype(BF16)
                coef_ref[o, at, h * LANES : (h + 1) * LANES] = coef
                z = z + jnp.dot(
                    coef, rows_ref[o, h * LANES : (h + 1) * LANES, :], preferred_element_type=F32
                )
            dt = softplus(z)
            dt_ref[o, at, :] = dt
            du_ref[o, at, :] = dt * act


def block_at(i, o, length):
    size = BLOCK * 8
    i = length // size - 1 - i if o == 1 else i
    return pl.multiple_of(i * size, size)


def totals_kernel(pieces, copies, first, place_ref, *refs):
    recs, (dtw_ref, bias_ref, rates_ref) = refs[:pieces], refs[pieces : pieces + 3]
    excl_ref, tot_ref, decay_ref, rows_ref = refs[pieces + 3 : pieces + 7]
    dt_ref, du_ref, coef_ref, wide_ref, spread_ref, bx_ref = refs[pieces + 7 :]
    length = dt_ref.shape[1]
    halves = coef_ref.shape[2] // LANES
    inner = dtw_ref.shape[2]
    slice_width = SLICE // halves
    shift = jnp.where(place_ref[1] == 0, 0, inner - slice_width * place_ref[1])
    lane = lane_iota((1, LANES))
    used = lane < SLICE if halves == 1 else (lane & (HALF - 1)) < slice_width

    def cut(values):
        return pltpu.roll(values, shift, 1)[:, :LANES]

    def paired(values):
        return values if halves == 1 else jnp.where(lane < HALF, values, pltpu.roll(values, HALF, 1))

    wide_ref[...] = jnp.zeros_like(wide_ref)
    for o in range(2):
        dtw = cut(dtw_ref[first + o].astype(F32))
        mark = OFF_LANE - o * EACH
        for h in range(halves):
            base = h * LANES
            mine = lane < HALF if h == 0 else lane >= HALF
            if halves == 1:
                wide_ref[o, :RANK, :] = dtw
                off = jnp.full((1, LANES), -1e30, F32)
            else:
                moved = dtw if h == 0 else pltpu.roll(dtw, HALF, 1)
                wide_ref[o, base : base + RANK, :] = jnp.where(mine, moved, 0.0)
                off = jnp.where(mine, -1e30, 0.0)
            wide_ref[o, base + mark : base + mark + 1, :] = off
        rows_ref[o] = wide_ref[o].astype(BF16)
        bias = cut(bias_ref[...])[first + o : first + o + 1]
        rates = cut(rates_ref[first + o])
        decay_ref[o, :STATE] = jnp.where(used, paired(rates) * -LOG2E, 0.0)
        decay_ref[o, STATE:] = jnp.broadcast_to(
            jnp.where(used, paired(bias), -1e30), (TOT - STATE, LANES)
        )
    bias = [decay_ref[o, STATE : STATE + 1, :] for o in range(2)]
    prepare(recs, place_ref[0], rows_ref, bias, dt_ref, du_ref, coef_ref)
    spread_matrix(spread_ref)
    sub = lax.broadcasted_iota(jnp.int32, (8, LANES), 0)
    spans = []
    for o in range(2):
        decay = [jnp.broadcast_to(decay_ref[o, n : n + 1, :], (8, LANES)) for n in range(STATE)]

        def advance(i, carry):
            span, states = carry
            states = list(states)
            base = block_at(i, o, length)
            bx_ref[...] = jnp.dot(
                coef_ref[o, pl.ds(base, BLOCK * 8), :], spread_ref[...], preferred_element_type=F32
            )
            for t in range(BLOCK) if o == 0 else range(BLOCK - 1, -1, -1):
                dt = dt_ref[o, pl.ds(base + t * 8, 8), :]
                du = du_ref[o, pl.ds(base + t * 8, 8), :]
                for n in range(STATE):
                    b = bx_ref[t * 8 : t * 8 + 8, n * LANES : (n + 1) * LANES]
                    states[n] = jnp.exp2(decay[n] * dt) * states[n] + du * b
                span = span + dt
            return span, tuple(states)

        zero = jnp.zeros((8, LANES), F32)
        span, states = lax.fori_loop(0, length // (8 * BLOCK), advance, (zero, (zero,) * STATE))
        states = list(states)
        for k in (1, 2, 4):
            shift_k = k if o == 0 else 8 - k
            keep = sub >= k if o == 0 else sub < 8 - k
            for n in range(STATE):
                moved = jnp.where(keep, pltpu.roll(states[n], shift_k, 0), 0.0)
                states[n] = jnp.exp2(decay[n] * span) * moved + states[n]
            span = span + jnp.where(keep, pltpu.roll(span, shift_k, 0), 0.0)
        shift_k = 1 if o == 0 else 7
        keep = sub >= 1 if o == 0 else sub < 7
        last = 7 if o == 0 else 0
        ends = jnp.concatenate([s[last : last + 1] for s in states], axis=0)
        end = span[last : last + 1]
        states = [jnp.where(keep, pltpu.roll(s, shift_k, 0), 0.0) for s in states]
        span = jnp.where(keep, pltpu.roll(span, shift_k, 0), 0.0)
        if halves == 2:
            second = lane >= HALF if o == 0 else lane < HALF
            before = pltpu.roll(ends, HALF, 1)
            for n in range(STATE):
                lifted = jnp.exp2(decay[n] * span) * before[n : n + 1] + states[n]
                states[n] = jnp.where(second, lifted, states[n])
            ends = jnp.exp2(decay_ref[o, :STATE] * end) * before + ends
            ends = jnp.where(second, ends, pltpu.roll(ends, HALF, 1))
            span = span + jnp.where(second, pltpu.roll(end, HALF, 1), 0.0)
            end = end + pltpu.roll(end, HALF, 1)
        for n in range(STATE):
            excl_ref[o, n] = states[n]
        excl_ref[o, STATE] = span
        high = end.astype(BF16).astype(F32)
        row = lax.broadcasted_iota(jnp.int32, (STATE, LANES), 0)
        spans.append(jnp.where(row == 2 * o, high, jnp.where(row == 2 * o + 1, end - high, 0.0)))
        for k in range(copies):
            tot_ref[k, o * STATE : (o + 1) * STATE, :] = ends.astype(BF16)
    for k in range(copies):
        tot_ref[k, 2 * STATE :, :] = (spans[0] + spans[1]).astype(BF16)


def outputs_kernel(pieces, parts_out, place_ref, gathered_ref, excl_ref, decay_ref, rows_ref, *refs):
    recs, outs = refs[:pieces], refs[pieces : pieces + parts_out]
    dt_ref, du_ref, coef_ref, spread_ref, bx_ref, sum_ref = refs[pieces + parts_out :]
    length = dt_ref.shape[1]
    chunks = gathered_ref.shape[0]
    bias = [decay_ref[o, STATE : STATE + 1, :] for o in range(2)]
    prepare(recs, place_ref[0], rows_ref, bias, dt_ref, du_ref, coef_ref)
    place = place_ref[2]
    spread_matrix(spread_ref)
    for o in range(2):
        rates = decay_ref[o, :STATE]
        entry = jnp.zeros((STATE, LANES), F32)
        for k in range(chunks) if o == 0 else range(chunks - 1, -1, -1):
            ahead = k < place if o == 0 else k > place
            tail = gathered_ref[k, 2 * STATE :, :].astype(F32)
            span = tail[2 * o : 2 * o + 1] + tail[2 * o + 1 : 2 * o + 2]
            ends = gathered_ref[k, o * STATE : (o + 1) * STATE, :].astype(F32)
            following = jnp.exp2(rates * span) * entry + ends
            entry = jnp.where(ahead, following, entry)
        decay = [jnp.broadcast_to(decay_ref[o, n : n + 1, :], (8, LANES)) for n in range(STATE)]
        states = tuple(
            jnp.exp2(decay[n] * excl_ref[o, STATE]) * entry[n : n + 1] + excl_ref[o, n]
            for n in range(STATE)
        )

        def advance(i, states):
            states = list(states)
            base = block_at(i, o, length)
            bx_ref[...] = jnp.dot(
                coef_ref[o, pl.ds(base, BLOCK * 8), :], spread_ref[...], preferred_element_type=F32
            )
            for t in range(BLOCK) if o == 0 else range(BLOCK - 1, -1, -1):
                at = pl.ds(base + t * 8, 8)
                dt = dt_ref[o, at, :]
                du = du_ref[o, at, :]
                parts = []
                for n in range(STATE):
                    b = bx_ref[t * 8 : t * 8 + 8, n * LANES : (n + 1) * LANES]
                    c = bx_ref[t * 8 : t * 8 + 8, (STATE + n) * LANES : (STATE + n + 1) * LANES]
                    states[n] = jnp.exp2(decay[n] * dt) * states[n] + du * b
                    parts.append(states[n] * c)
                while len(parts) > 1:
                    parts = [a + b for a, b in zip(parts[::2], parts[1::2])]
                if o == 0:
                    sum_ref[at, :] = parts[0]
                else:
                    sum_ref[at, :] = sum_ref[at, :] + parts[0]
            return tuple(states)

        lax.fori_loop(0, length // (8 * BLOCK), advance, states)
    if parts_out == 1:
        outs[0][...] = sum_ref[...].astype(BF16)
    else:
        step = length // 8
        for flip in range(2):
            for j in range(4):
                at = pl.multiple_of(column(place_ref[0], j, flip) * step, step)
                outs[flip][j] = sum_ref[pl.ds(at, step), :].astype(BF16)


def final_kernel(
    place_ref, yc_ref, act_ref, gate_ref, skip_ref, gain_ref, w_ref, live_ref, *refs
):
    yr_refs, out_ref, slices_ref = refs[:4], refs[4], refs[5]
    turn = order_matrix(False)
    for j in range(4):
        for flip in range(2):
            slices_ref[column(place_ref[0], -j, flip)] = yr_refs[j][flip]
    parts = [jnp.dot(turn, slices_ref[k], preferred_element_type=F32) for k in range(8)]
    narrow = [yc_ref[k].astype(F32) for k in range(16)]
    sides = [
        jnp.concatenate(join_narrow(narrow, HALF * h), axis=1).reshape(8, 8, -1) for h in range(2)
    ]
    combined = jnp.concatenate(join_slices(parts), axis=1)
    combined = combined + jnp.concatenate(sides, axis=1).reshape(combined.shape)
    combined = combined + skip_ref[...] * act_ref[...].astype(F32)
    mean = jnp.mean(combined, axis=1, keepdims=True)
    centered = combined - mean
    variance = jnp.mean(centered * centered, axis=1, keepdims=True)
    normed = centered * lax.rsqrt(variance + 1e-05) * gain_ref[...]
    mixed = (normed * silu(gate_ref[...].astype(F32))).astype(BF16)
    out_ref[...] = (
        jnp.dot(mixed, w_ref[...], preferred_element_type=F32) * live_ref[...]
    ).astype(BF16)


def shifted(values, axis, step):
    count = lax.axis_size(axis)
    pairs = [(i, i + step) for i in range(count) if 0 <= i + step < count]
    return lax.ppermute(values, axis, pairs)


def exchange(near, far):
    count = lax.axis_size("col")
    merged = call(
        merge_kernel,
        (jax.ShapeDtypeStruct((2,) + near.shape[1:], near.dtype),) * 4,
        vmem(2),
        flops=10**6,
        name="merge",
    )(near, far)
    return [
        m if j == 0 else lax.ppermute(m, "col", [(c, (c + 2 * j) % count) for c in range(count)])
        for j, m in enumerate(merged)
    ]


def crossed(far):
    return lax.ppermute(far, "col", [(c, c ^ 1) for c in range(lax.axis_size("col"))])


def per_device(
    patches, tissue, in_weight, conv_weight, conv_bias, x_weight, dt_weight, dt_bias,
    decay_rate, skip_gain, norm_gain, out_weight,
):
    tile_rows, tile_cols, channels = patches.shape
    inner = out_weight.shape[0]
    tokens = tile_rows * tile_cols
    row = lax.axis_index("row").astype(jnp.int32)
    col = lax.axis_index("col").astype(jnp.int32)
    place_r = jnp.stack([col, col, row])
    place_c = jnp.stack([col, row, col])
    top = shifted(patches[-1], "row", 1)
    bottom = shifted(patches[0], "row", -1)

    def edge(j):
        return jnp.concatenate([top[j : j + 1], patches[:, j], bottom[j : j + 1]], axis=0)

    left = shifted(edge(tile_cols - 1), "col", 1)
    right = shifted(edge(0), "col", -1)
    projected = jnp.dot(
        patches.reshape(tokens, channels), in_weight, preferred_element_type=F32
    ).astype(BF16)
    x_inner = projected[:, :inner]
    gate = projected[:, inner:]
    live = tissue.reshape(tokens, 1).astype(F32)
    rates = jnp.swapaxes(decay_rate, 1, 2)

    smem = [pl.BlockSpec(memory_space=pltpu.SMEM)]
    outs = call(
        local_kernel,
        (jax.ShapeDtypeStruct((tokens, inner), BF16),)
        + (jax.ShapeDtypeStruct((4, tokens, 2 * LANES), BF16),) * 2
        + (jax.ShapeDtypeStruct((16, tokens // 2, 3 * LANES), BF16),),
        smem + vmem(10),
        [
            pltpu.VMEM((10, 32, inner), F32),
            pltpu.VMEM((inner, 2 * LANES), BF16),
            pltpu.VMEM((8, tokens, LANES), BF16),
        ],
        name="local",
    )(
        place_r, x_inner, top, bottom, left, right, in_weight,
        conv_weight.reshape(9, inner), conv_bias.reshape(1, inner), x_weight, 1.0 - live,
    )
    act, near_r, far_r, rec_c = outs
    length = 8 * tokens
    wide = (length, LANES)


    def scratch(halves):
        return [
            pltpu.VMEM((2,) + wide, F32),
            pltpu.VMEM((2,) + wide, F32),
            pltpu.VMEM((2, length, halves * LANES), BF16),
        ]

    def totals(place, recs, copies, first, halves, name):
        return call(
            functools.partial(totals_kernel, len(recs), copies, first),
            (
                jax.ShapeDtypeStruct((2, STATE + 1, 8, LANES), F32),
                jax.ShapeDtypeStruct((copies, 3 * STATE, LANES), BF16),
                jax.ShapeDtypeStruct((2, TOT, LANES), F32),
                jax.ShapeDtypeStruct((2, halves * LANES, LANES), BF16),
            ),
            smem + vmem(len(recs) + 3),
            scratch(halves)
            + [
                pltpu.VMEM((2, halves * LANES, LANES), F32),
                pltpu.VMEM((halves * LANES, STATE * LANES), BF16),
                pltpu.VMEM((8 * BLOCK, STATE * LANES), F32),
            ],
            flops=10**9,
            grant=20,
            name=name,
        )(place, *recs, dt_weight, dt_bias, rates)

    def outputs(place, tot, excl, decay, rows, recs, out, halves, name):
        return call(
            functools.partial(outputs_kernel, len(recs), len(out)),
            out,
            smem + vmem(len(recs) + 4),
            scratch(halves)
            + [
                pltpu.VMEM((halves * LANES, 2 * STATE * LANES), BF16),
                pltpu.VMEM((8 * BLOCK, 2 * STATE * LANES), F32),
                pltpu.VMEM(wide, F32),
            ],
            flops=10**9,
            grant=24,
            name=name,
        )(place, tot, excl, decay, rows, *recs)

    rec_r = exchange(near_r, crossed(far_r))
    rec_c = lax.all_to_all(rec_c, "row", 0, 0).reshape(length, 3 * LANES)

    excl_r, tot_r, decay_r, rows_r = totals(place_r, rec_r, 16, 0, 1, "totals_rows")
    excl_c, tot_c, decay_c, rows_c = totals(place_c, [rec_c], 8, 2, 2, "totals_cols")

    tot_r = lax.all_to_all(tot_r, "row", 0, 0)
    tot_c = lax.all_to_all(tot_c, "col", 0, 0)

    near_y, far_y = outputs(
        place_r, tot_r, excl_r, decay_r, rows_r, rec_r,
        (jax.ShapeDtypeStruct((4, tokens, LANES), BF16),) * 2, 1, "outputs_rows",
    )
    (y_c,) = outputs(
        place_c, tot_c, excl_c, decay_c, rows_c, [rec_c],
        (jax.ShapeDtypeStruct(wide, BF16),), 2, "outputs_cols",
    )
    y_c, far_y = lax.optimization_barrier((y_c, crossed(far_y)))
    y_r = exchange(near_y, far_y)
    y_c = lax.all_to_all(y_c.reshape(16, tokens // 2, LANES), "row", 0, 0)

    result = call(
        final_kernel,
        jax.ShapeDtypeStruct((tokens, channels), BF16),
        smem + vmem(11),
        [pltpu.VMEM((8, tokens, LANES), BF16)],
        name="final",
    )(
        place_r, y_c, act, gate, skip_gain.reshape(1, inner), norm_gain.reshape(1, inner),
        out_weight, live, *y_r,
    )
    return result.reshape(tile_rows, tile_cols, channels)


def solution(mesh):
    in_specs = (P("row", "col", None), P("row", "col")) + (P(),) * 10
    return jax.shard_map(
        per_device, mesh=mesh, in_specs=in_specs, out_specs=P("row", "col", None), check_vma=False
    )
```

```python
import functools
import math

import jax
import jax.numpy as jnp
from jax import lax
from jax.experimental import pallas as pl
from jax.experimental.pallas import tpu as pltpu
from jax.sharding import PartitionSpec as P

F32 = jnp.float32
BF16 = jnp.bfloat16
LANES = 128
SLICE = 96
STATE = 16
RANK = 24
EACH = RANK + 2 * STATE
OFF_LANE = 2 * EACH
TOT = 24
BLOCK = 64
LOG2E = math.log2(math.e)
HALF = 64


def vmem(count):
    return [pl.BlockSpec(memory_space=pltpu.VMEM)] * count


def call(kernel, out_shape, in_specs, scratch=(), flops=10**7, grant=16, name=None):
    return pl.pallas_call(
        kernel,
        out_shape=out_shape,
        in_specs=in_specs,
        out_specs=jax.tree.map(lambda _: pl.BlockSpec(memory_space=pltpu.VMEM), out_shape),
        scratch_shapes=list(scratch),
        compiler_params=pltpu.CompilerParams(vmem_limit_bytes=grant << 20),
        cost_estimate=pl.CostEstimate(flops=flops, bytes_accessed=4 * 10**6, transcendentals=0),
        name=name,
    )


def lane_iota(shape):
    return lax.broadcasted_iota(jnp.int32, shape, len(shape) - 1)


def softplus(x):
    u = jnp.exp2(jnp.abs(x) * -LOG2E)
    series = u * (1.0 - u * (0.5 - u * (1.0 / 3.0 - u * 0.25)))
    return jnp.maximum(x, 0.0) + jnp.where(u < 0.03, series, jnp.log(1.0 + u))


def silu(x):
    return x * jax.nn.sigmoid(x)


def cut_slice(values, k):
    j0, off = divmod(SLICE * k, LANES)
    first = values[:, j0 * LANES : (j0 + 1) * LANES]
    if off == 0:
        return first
    shift = LANES - off
    head = pltpu.roll(first, shift, 1)
    if shift >= SLICE:
        return head
    second = values[:, (j0 + 1) * LANES : (j0 + 2) * LANES]
    tail = pltpu.roll(second, shift, 1)
    return jnp.where(lane_iota(head.shape) < shift, head, tail)


def join_slices(parts):
    tiles = []
    lane = lane_iota(parts[0].shape)
    for m in range(2):
        y0, y1, y2, y3 = parts[4 * m : 4 * m + 4]
        r1 = pltpu.roll(y1, 96, 1)
        r2 = pltpu.roll(y2, 64, 1)
        r3 = pltpu.roll(y3, 32, 1)
        tiles.append(jnp.where(lane < 96, y0, r1))
        tiles.append(jnp.where(lane < 64, r1, r2))
        tiles.append(jnp.where(lane < 32, r2, r3))
    return tiles


def cut_narrow(values, k, start):
    j0, off = divmod(SLICE // 2 * k, LANES)
    shift = (start - off) % LANES
    first = values[:, j0 * LANES : (j0 + 1) * LANES]
    head = first if shift == 0 else pltpu.roll(first, shift, 1)
    if off + SLICE // 2 <= LANES:
        return head
    second = values[:, (j0 + 1) * LANES : (j0 + 2) * LANES]
    tail = pltpu.roll(second, shift, 1)
    return jnp.where(lane_iota(head.shape) < start + LANES - off, head, tail)


def join_narrow(parts, start):
    lane = lane_iota(parts[0].shape)

    def pick(chosen, bounds):
        out = chosen[-1]
        for value, bound in zip(chosen[-2::-1], bounds[::-1]):
            out = jnp.where(lane < bound, value, out)
        return out

    tiles = []
    for m in range(2):
        r = []
        for k in range(8):
            shift = (48 * k - start) % LANES
            y = parts[8 * m + k]
            r.append(y if shift == 0 else pltpu.roll(y, shift, 1))
        tiles.append(pick(r[0:3], (48, 96)))
        tiles.append(pick(r[2:6], (16, 64, 112)))
        tiles.append(pick(r[5:8], (32, 80)))
    return tiles


def order_matrix(to_columns):
    q = lax.broadcasted_iota(jnp.int32, (LANES, LANES), 0 if to_columns else 1)
    p = lax.broadcasted_iota(jnp.int32, (LANES, LANES), 1 if to_columns else 0)
    return (p == (q % 8) * 16 + q // 8).astype(F32).astype(BF16)


def column(col, chips, flip):
    return ((col + 2 * chips) & 7) ^ flip


def merge_kernel(near_ref, far_ref, *out_refs):
    for j, out_ref in enumerate(out_refs):
        out_ref[0] = near_ref[j]
        out_ref[1] = far_ref[j]


def local_kernel(
    place_ref, x_ref, row_near_ref, row_away_ref, col_near_ref, col_away_ref, w_ref, cw_ref, cb_ref, xw_ref, off_ref,
    *rest,
):
    act_ref, near_ref, far_ref, recc_ref, frame_ref, xwide_ref, slices_ref = rest
    inner = x_ref.shape[1]
    weight = w_ref[:, :inner]

    def project(v):
        return jnp.dot(v, weight, preferred_element_type=F32).astype(BF16).astype(F32)

    frame_ref[1:9, 8:24, :] = x_ref[...].astype(F32).reshape(8, 16, inner)
    rows = (project(row_near_ref[...]), project(row_away_ref[...]))
    top, bottom = before_after(rows, (place_ref[2] & 1) == 0)
    frame_ref[0:1, 8:24, :] = top.reshape(1, 16, inner)
    frame_ref[9:10, 8:24, :] = bottom.reshape(1, 16, inner)
    cols = (project(col_near_ref[...]), project(col_away_ref[...]))
    left, right = before_after(cols, (place_ref[0] & 1) == 0)
    for i in range(10):
        frame_ref[i, 7:8, :] = left[i : i + 1]
        frame_ref[i, 24:25, :] = right[i : i + 1]
    total = jnp.zeros((8, 16, inner), F32) + cb_ref[...].reshape(1, 1, inner)
    for dc in range(3):
        for dr in range(3):
            k = dr * 3 + dc
            total = total + frame_ref[dr : dr + 8, 7 + dc : 23 + dc, :] * cw_ref[
                k : k + 1, :
            ].reshape(1, 1, inner)
    act = silu(total).reshape(LANES, inner).astype(BF16)
    act_ref[...] = act
    xwide_ref[:, LANES:] = jnp.zeros((inner, LANES), BF16)
    xwide_ref[:, : xw_ref.shape[1]] = xw_ref[...]
    coef = jnp.dot(act, xwide_ref[...], preferred_element_type=F32)
    lane = lane_iota((LANES, LANES))
    off = jnp.broadcast_to(off_ref[...], (LANES, LANES))
    coef_r = jnp.where(lane == OFF_LANE, off, jnp.where(lane < OFF_LANE, coef[:, :LANES], 0.0)).astype(BF16)
    coef_c = pltpu.roll(jnp.where(lane >= OFF_LANE, coef[:, :LANES], coef[:, LANES:]), 16, 1)
    coef_c = jnp.where(lane == OFF_LANE, off, jnp.where(lane < OFF_LANE, coef_c, 0.0))
    turn = order_matrix(True)
    act_r = jnp.dot(turn, act, preferred_element_type=F32)
    coef_r = jnp.dot(turn, coef_r, preferred_element_type=F32).astype(BF16)
    wide = act.astype(F32).reshape(8, 16, inner)
    half = coef_c.reshape(8, 16, LANES)
    sides = [wide[:, 8 * h : 8 * h + 8, :].reshape(HALF, inner) for h in range(2)]
    coefs = [half[:, 8 * h : 8 * h + 8, :].reshape(HALF, LANES).astype(BF16) for h in range(2)]
    for k in range(8):
        slices_ref[k] = cut_slice(act_r, k).astype(BF16)
    for k in range(16):
        pair = [cut_narrow(sides[h], k, HALF * h) for h in range(2)]
        recc_ref[k, :, :LANES] = jnp.where(
            lane_iota(pair[0].shape) < HALF, pair[0], pair[1]
        ).astype(BF16)
        for h in range(2):
            recc_ref[k, :, (1 + h) * LANES : (2 + h) * LANES] = coefs[h]
    for ref, flip in ((near_ref, 0), (far_ref, 1)):
        for j in range(4):
            ref[j, :, :LANES] = slices_ref[column(place_ref[0], j, flip)]
            ref[j, :, LANES:] = coef_r


def spread_matrix(spread_ref):
    halves = spread_ref.shape[0] // LANES
    low, high = 16, 64
    spread_ref[...] = jnp.zeros_like(spread_ref)
    shape = (high - low, spread_ref.shape[1])
    source = lax.broadcasted_iota(jnp.int32, shape, 0) + low
    place = lax.broadcasted_iota(jnp.int32, shape, 1)
    hit = source == RANK + place // LANES
    for h in range(halves):
        side = hit if halves == 1 else jnp.logical_and(hit, ((place // HALF) & 1) == h)
        spread_ref[h * LANES + low : h * LANES + high, :] = side.astype(F32).astype(BF16)


def prepare(recs, place, rows_ref, bias, dt_ref, du_ref, coef_ref):
    length = dt_ref.shape[1]
    halves = coef_ref.shape[2] // LANES
    size = length // 8
    for j in range(8):
        if len(recs) == 1:
            rec = recs[0].at[j * size : (j + 1) * size]
            at = pl.ds(j * size, size)
        else:
            rec = recs[j // 2].at[j % 2]
            at = pl.ds(pl.multiple_of(column(place, -(j // 2), j % 2) * size, size), size)
        act = rec[:, :LANES].astype(F32)
        for o in range(2):
            z = bias[o]
            for h in range(halves):
                coef = rec[:, (1 + h) * LANES : (2 + h) * LANES]
                if o == 1:
                    coef = pltpu.roll(coef.astype(F32), LANES - EACH, 1).astype(BF16)
                coef_ref[o, at, h * LANES : (h + 1) * LANES] = coef
                z = z + jnp.dot(
                    coef, rows_ref[o, h * LANES : (h + 1) * LANES, :], preferred_element_type=F32
                )
            dt = softplus(z)
            dt_ref[o, at, :] = dt
            du_ref[o, at, :] = dt * act


def block_at(i, o, length):
    size = BLOCK * 8
    i = length // size - 1 - i if o == 1 else i
    return pl.multiple_of(i * size, size)


def totals_kernel(pieces, copies, first, place_ref, *refs):
    recs, (dtw_ref, bias_ref, rates_ref) = refs[:pieces], refs[pieces : pieces + 3]
    excl_ref, tot_ref, decay_ref, rows_ref = refs[pieces + 3 : pieces + 7]
    dt_ref, du_ref, coef_ref, wide_ref, spread_ref, bx_ref = refs[pieces + 7 :]
    length = dt_ref.shape[1]
    halves = coef_ref.shape[2] // LANES
    inner = dtw_ref.shape[2]
    slice_width = SLICE // halves
    shift = jnp.where(place_ref[1] == 0, 0, inner - slice_width * place_ref[1])
    lane = lane_iota((1, LANES))
    used = lane < SLICE if halves == 1 else (lane & (HALF - 1)) < slice_width

    def cut(values):
        return pltpu.roll(values, shift, 1)[:, :LANES]

    def paired(values):
        return values if halves == 1 else jnp.where(lane < HALF, values, pltpu.roll(values, HALF, 1))

    wide_ref[...] = jnp.zeros_like(wide_ref)
    for o in range(2):
        dtw = cut(dtw_ref[first + o].astype(F32))
        mark = OFF_LANE - o * EACH
        for h in range(halves):
            base = h * LANES
            mine = lane < HALF if h == 0 else lane >= HALF
            if halves == 1:
                wide_ref[o, :RANK, :] = dtw
                off = jnp.full((1, LANES), -1e30, F32)
            else:
                moved = dtw if h == 0 else pltpu.roll(dtw, HALF, 1)
                wide_ref[o, base : base + RANK, :] = jnp.where(mine, moved, 0.0)
                off = jnp.where(mine, -1e30, 0.0)
            wide_ref[o, base + mark : base + mark + 1, :] = off
        rows_ref[o] = wide_ref[o].astype(BF16)
        bias = cut(bias_ref[...])[first + o : first + o + 1]
        rates = cut(rates_ref[first + o])
        decay_ref[o, :STATE] = jnp.where(used, paired(rates) * -LOG2E, 0.0)
        decay_ref[o, STATE:] = jnp.broadcast_to(
            jnp.where(used, paired(bias), -1e30), (TOT - STATE, LANES)
        )
    bias = [decay_ref[o, STATE : STATE + 1, :] for o in range(2)]
    prepare(recs, place_ref[0], rows_ref, bias, dt_ref, du_ref, coef_ref)
    spread_matrix(spread_ref)
    sub = lax.broadcasted_iota(jnp.int32, (8, LANES), 0)
    spans = []
    for o in range(2):
        decay = [jnp.broadcast_to(decay_ref[o, n : n + 1, :], (8, LANES)) for n in range(STATE)]

        def advance(i, carry):
            span, states = carry
            states = list(states)
            base = block_at(i, o, length)
            bx_ref[...] = jnp.dot(
                coef_ref[o, pl.ds(base, BLOCK * 8), :], spread_ref[...], preferred_element_type=F32
            )
            for t in range(BLOCK) if o == 0 else range(BLOCK - 1, -1, -1):
                dt = dt_ref[o, pl.ds(base + t * 8, 8), :]
                du = du_ref[o, pl.ds(base + t * 8, 8), :]
                for n in range(STATE):
                    b = bx_ref[t * 8 : t * 8 + 8, n * LANES : (n + 1) * LANES]
                    states[n] = jnp.exp2(decay[n] * dt) * states[n] + du * b
                span = span + dt
            return span, tuple(states)

        zero = jnp.zeros((8, LANES), F32)
        span, states = lax.fori_loop(0, length // (8 * BLOCK), advance, (zero, (zero,) * STATE))
        states = list(states)
        for k in (1, 2, 4):
            shift_k = k if o == 0 else 8 - k
            keep = sub >= k if o == 0 else sub < 8 - k
            for n in range(STATE):
                moved = jnp.where(keep, pltpu.roll(states[n], shift_k, 0), 0.0)
                states[n] = jnp.exp2(decay[n] * span) * moved + states[n]
            span = span + jnp.where(keep, pltpu.roll(span, shift_k, 0), 0.0)
        shift_k = 1 if o == 0 else 7
        keep = sub >= 1 if o == 0 else sub < 7
        last = 7 if o == 0 else 0
        ends = jnp.concatenate([s[last : last + 1] for s in states], axis=0)
        end = span[last : last + 1]
        states = [jnp.where(keep, pltpu.roll(s, shift_k, 0), 0.0) for s in states]
        span = jnp.where(keep, pltpu.roll(span, shift_k, 0), 0.0)
        if halves == 2:
            second = lane >= HALF if o == 0 else lane < HALF
            before = pltpu.roll(ends, HALF, 1)
            for n in range(STATE):
                lifted = jnp.exp2(decay[n] * span) * before[n : n + 1] + states[n]
                states[n] = jnp.where(second, lifted, states[n])
            ends = jnp.exp2(decay_ref[o, :STATE] * end) * before + ends
            ends = jnp.where(second, ends, pltpu.roll(ends, HALF, 1))
            span = span + jnp.where(second, pltpu.roll(end, HALF, 1), 0.0)
            end = end + pltpu.roll(end, HALF, 1)
        for n in range(STATE):
            excl_ref[o, n] = states[n]
        excl_ref[o, STATE] = span
        high = end.astype(BF16).astype(F32)
        row = lax.broadcasted_iota(jnp.int32, (STATE, LANES), 0)
        spans.append(jnp.where(row == 2 * o, high, jnp.where(row == 2 * o + 1, end - high, 0.0)))
        for k in range(copies):
            tot_ref[k, o * STATE : (o + 1) * STATE, :] = ends.astype(BF16)
    for k in range(copies):
        tot_ref[k, 2 * STATE :, :] = (spans[0] + spans[1]).astype(BF16)


def outputs_kernel(pieces, parts_out, place_ref, gathered_ref, excl_ref, decay_ref, rows_ref, *refs):
    recs, outs = refs[:pieces], refs[pieces : pieces + parts_out]
    dt_ref, du_ref, coef_ref, spread_ref, bx_ref, sum_ref = refs[pieces + parts_out :]
    length = dt_ref.shape[1]
    chunks = gathered_ref.shape[0]
    bias = [decay_ref[o, STATE : STATE + 1, :] for o in range(2)]
    prepare(recs, place_ref[0], rows_ref, bias, dt_ref, du_ref, coef_ref)
    place = place_ref[2]
    spread_matrix(spread_ref)
    for o in range(2):
        rates = decay_ref[o, :STATE]
        entry = jnp.zeros((STATE, LANES), F32)
        for k in range(chunks) if o == 0 else range(chunks - 1, -1, -1):
            ahead = k < place if o == 0 else k > place
            tail = gathered_ref[k, 2 * STATE :, :].astype(F32)
            span = tail[2 * o : 2 * o + 1] + tail[2 * o + 1 : 2 * o + 2]
            ends = gathered_ref[k, o * STATE : (o + 1) * STATE, :].astype(F32)
            following = jnp.exp2(rates * span) * entry + ends
            entry = jnp.where(ahead, following, entry)
        decay = [jnp.broadcast_to(decay_ref[o, n : n + 1, :], (8, LANES)) for n in range(STATE)]
        states = tuple(
            jnp.exp2(decay[n] * excl_ref[o, STATE]) * entry[n : n + 1] + excl_ref[o, n]
            for n in range(STATE)
        )

        def advance(i, states):
            states = list(states)
            base = block_at(i, o, length)
            bx_ref[...] = jnp.dot(
                coef_ref[o, pl.ds(base, BLOCK * 8), :], spread_ref[...], preferred_element_type=F32
            )
            for t in range(BLOCK) if o == 0 else range(BLOCK - 1, -1, -1):
                at = pl.ds(base + t * 8, 8)
                dt = dt_ref[o, at, :]
                du = du_ref[o, at, :]
                parts = []
                for n in range(STATE):
                    b = bx_ref[t * 8 : t * 8 + 8, n * LANES : (n + 1) * LANES]
                    c = bx_ref[t * 8 : t * 8 + 8, (STATE + n) * LANES : (STATE + n + 1) * LANES]
                    states[n] = jnp.exp2(decay[n] * dt) * states[n] + du * b
                    parts.append(states[n] * c)
                while len(parts) > 1:
                    parts = [a + b for a, b in zip(parts[::2], parts[1::2])]
                if o == 0:
                    sum_ref[at, :] = parts[0]
                else:
                    sum_ref[at, :] = sum_ref[at, :] + parts[0]
            return tuple(states)

        lax.fori_loop(0, length // (8 * BLOCK), advance, states)
    if parts_out == 1:
        outs[0][...] = sum_ref[...].astype(BF16)
    else:
        step = length // 8
        for flip in range(2):
            for j in range(4):
                at = pl.multiple_of(column(place_ref[0], j, flip) * step, step)
                outs[flip][j] = sum_ref[pl.ds(at, step), :].astype(BF16)


def final_kernel(
    place_ref, yc_ref, act_ref, gate_ref, skip_ref, gain_ref, w_ref, live_ref, *refs
):
    yr_refs, out_ref, slices_ref = refs[:4], refs[4], refs[5]
    turn = order_matrix(False)
    for j in range(4):
        for flip in range(2):
            slices_ref[column(place_ref[0], -j, flip)] = yr_refs[j][flip]
    parts = [jnp.dot(turn, slices_ref[k], preferred_element_type=F32) for k in range(8)]
    narrow = [yc_ref[k].astype(F32) for k in range(16)]
    sides = [
        jnp.concatenate(join_narrow(narrow, HALF * h), axis=1).reshape(8, 8, -1) for h in range(2)
    ]
    combined = jnp.concatenate(join_slices(parts), axis=1)
    combined = combined + jnp.concatenate(sides, axis=1).reshape(combined.shape)
    combined = combined + skip_ref[...] * act_ref[...].astype(F32)
    mean = jnp.mean(combined, axis=1, keepdims=True)
    centered = combined - mean
    variance = jnp.mean(centered * centered, axis=1, keepdims=True)
    normed = centered * lax.rsqrt(variance + 1e-05) * gain_ref[...]
    mixed = (normed * silu(gate_ref[...].astype(F32))).astype(BF16)
    out_ref[...] = (
        jnp.dot(mixed, w_ref[...], preferred_element_type=F32) * live_ref[...]
    ).astype(BF16)


def swapped(low, high, axis):
    count = lax.axis_size(axis)
    even = lax.axis_index(axis) % 2 == 0
    inner = [(i, i ^ 1) for i in range(count)]
    outer = [(i + d, i + 1 - d) for i in range(1, count - 1, 2) for d in range(2)]
    near = lax.ppermute(jnp.where(even, high, low), axis, inner)
    away = lax.ppermute(jnp.where(even, low, high), axis, outer)
    return near, away


def before_after(pair, even):
    near, away = pair
    return jnp.where(even, away, near), jnp.where(even, near, away)


def exchange(near, far):
    count = lax.axis_size("col")
    merged = call(
        merge_kernel,
        (jax.ShapeDtypeStruct((2,) + near.shape[1:], near.dtype),) * 4,
        vmem(2),
        flops=10**6,
        name="merge",
    )(near, far)
    return [
        m if j == 0 else lax.ppermute(m, "col", [(c, (c + 2 * j) % count) for c in range(count)])
        for j, m in enumerate(merged)
    ]


def crossed(far):
    return lax.ppermute(far, "col", [(c, c ^ 1) for c in range(lax.axis_size("col"))])


def per_device(
    patches, tissue, in_weight, conv_weight, conv_bias, x_weight, dt_weight, dt_bias,
    decay_rate, skip_gain, norm_gain, out_weight,
):
    tile_rows, tile_cols, channels = patches.shape
    inner = out_weight.shape[0]
    tokens = tile_rows * tile_cols
    row = lax.axis_index("row").astype(jnp.int32)
    col = lax.axis_index("col").astype(jnp.int32)
    place_r = jnp.stack([col, col, row])
    place_c = jnp.stack([col, row, col])
    row_pair = swapped(patches[0], patches[-1], "row")
    top, bottom = before_after(row_pair, row % 2 == 0)

    def edge(j):
        return jnp.concatenate([top[j : j + 1], patches[:, j], bottom[j : j + 1]], axis=0)

    col_pair = swapped(edge(0), edge(tile_cols - 1), "col")
    projected = jnp.dot(
        patches.reshape(tokens, channels), in_weight, preferred_element_type=F32
    ).astype(BF16)
    x_inner = projected[:, :inner]
    gate = projected[:, inner:]
    live = tissue.reshape(tokens, 1).astype(F32)
    rates = jnp.swapaxes(decay_rate, 1, 2)

    smem = [pl.BlockSpec(memory_space=pltpu.SMEM)]
    outs = call(
        local_kernel,
        (jax.ShapeDtypeStruct((tokens, inner), BF16),)
        + (jax.ShapeDtypeStruct((4, tokens, 2 * LANES), BF16),) * 2
        + (jax.ShapeDtypeStruct((16, tokens // 2, 3 * LANES), BF16),),
        smem + vmem(10),
        [
            pltpu.VMEM((10, 32, inner), F32),
            pltpu.VMEM((inner, 2 * LANES), BF16),
            pltpu.VMEM((8, tokens, LANES), BF16),
        ],
        name="local",
    )(
        place_r, x_inner, *row_pair, *col_pair, in_weight,
        conv_weight.reshape(9, inner), conv_bias.reshape(1, inner), x_weight, 1.0 - live,
    )
    act, near_r, far_r, rec_c = outs
    length = 8 * tokens
    wide = (length, LANES)


    def scratch(halves):
        return [
            pltpu.VMEM((2,) + wide, F32),
            pltpu.VMEM((2,) + wide, F32),
            pltpu.VMEM((2, length, halves * LANES), BF16),
        ]

    def totals(place, recs, copies, first, halves, name):
        return call(
            functools.partial(totals_kernel, len(recs), copies, first),
            (
                jax.ShapeDtypeStruct((2, STATE + 1, 8, LANES), F32),
                jax.ShapeDtypeStruct((copies, 3 * STATE, LANES), BF16),
                jax.ShapeDtypeStruct((2, TOT, LANES), F32),
                jax.ShapeDtypeStruct((2, halves * LANES, LANES), BF16),
            ),
            smem + vmem(len(recs) + 3),
            scratch(halves)
            + [
                pltpu.VMEM((2, halves * LANES, LANES), F32),
                pltpu.VMEM((halves * LANES, STATE * LANES), BF16),
                pltpu.VMEM((8 * BLOCK, STATE * LANES), F32),
            ],
            flops=10**9,
            grant=20,
            name=name,
        )(place, *recs, dt_weight, dt_bias, rates)

    def outputs(place, tot, excl, decay, rows, recs, out, halves, name):
        return call(
            functools.partial(outputs_kernel, len(recs), len(out)),
            out,
            smem + vmem(len(recs) + 4),
            scratch(halves)
            + [
                pltpu.VMEM((halves * LANES, 2 * STATE * LANES), BF16),
                pltpu.VMEM((8 * BLOCK, 2 * STATE * LANES), F32),
                pltpu.VMEM(wide, F32),
            ],
            flops=10**9,
            grant=24,
            name=name,
        )(place, tot, excl, decay, rows, *recs)

    rec_r = exchange(near_r, crossed(far_r))
    rec_c = lax.all_to_all(rec_c, "row", 0, 0).reshape(length, 3 * LANES)

    excl_r, tot_r, decay_r, rows_r = totals(place_r, rec_r, 16, 0, 1, "totals_rows")
    excl_c, tot_c, decay_c, rows_c = totals(place_c, [rec_c], 8, 2, 2, "totals_cols")

    tot_r = lax.all_to_all(tot_r, "row", 0, 0)
    tot_c = lax.all_to_all(tot_c, "col", 0, 0)

    near_y, far_y = outputs(
        place_r, tot_r, excl_r, decay_r, rows_r, rec_r,
        (jax.ShapeDtypeStruct((4, tokens, LANES), BF16),) * 2, 1, "outputs_rows",
    )
    (y_c,) = outputs(
        place_c, tot_c, excl_c, decay_c, rows_c, [rec_c],
        (jax.ShapeDtypeStruct(wide, BF16),), 2, "outputs_cols",
    )
    y_c, far_y = lax.optimization_barrier((y_c, crossed(far_y)))
    y_r = exchange(near_y, far_y)
    y_c = lax.all_to_all(y_c.reshape(16, tokens // 2, LANES), "row", 0, 0)

    result = call(
        final_kernel,
        jax.ShapeDtypeStruct((tokens, channels), BF16),
        smem + vmem(11),
        [pltpu.VMEM((8, tokens, LANES), BF16)],
        name="final",
    )(
        place_r, y_c, act, gate, skip_gain.reshape(1, inner), norm_gain.reshape(1, inner),
        out_weight, live, *y_r,
    )
    return result.reshape(tile_rows, tile_cols, channels)


def solution(mesh):
    in_specs = (P("row", "col", None), P("row", "col")) + (P(),) * 10
    return jax.shard_map(
        per_device, mesh=mesh, in_specs=in_specs, out_specs=P("row", "col", None), check_vma=False
    )
```
